32 devices in a mesh: seq: 8 (over z, y), chan: 4 (over x, core).
Axes of the slice: x: 2, y: 2, z: 4, core: 2. Of those that a mesh axis runs over, the one named last changes fastest.
Arguments:
- features: bfloat16 [2048, 3, 8192], P(('seq', 'chan')), may hold values from -6 to 6
- cotangent: bfloat16 [2048, 8192], P('seq', 'chan'), may hold values from -6 to 6
- short_filter: float32 [3, 512, 7], P(None, 'chan'), may hold values from -2.5 to 2.5
- medium_filter: float32 [512, 128], P('chan'), may hold values from -0.5 to 0.5
- doc_start: int32 [8], replicated, may hold values from 0 to 255
Outputs:
- hyena_out: bfloat16 [2048, 8192], P('seq', 'chan')
- feature_grad: bfloat16 [2048, 3, 8192], P(('seq', 'chan'))
The draws below stay inside these ranges and needn't reach their ends.
Inputs may be any that keep to these rules, and one draw needn't show every extreme that they name: Each shard holds exactly one document start, at position doc_start[i] of its 256 positions.
All inputs are finite; a program needn't handle non-finite values.
Results may differ from the reference program's by a relative error of at most 0.006.
Values may be sent and summed in bfloat16 or wider, within the bound.
A program may use at most 128 MiB of HBM per device.

```python
import jax
import jax.numpy as jnp
from jax import lax

D = 8192
GROUPS = 512
SHORT = 7
MEDIUM = 128
TOK_DEV = 256
TOKENS = 2048
SHARDS = 8


def with_ends(array, key, smallest, largest):
    shape = array.shape
    index_at = [jax.random.randint(jax.random.fold_in(key, axis), (), 0, shape[axis]) for axis in range(len(shape))]
    array = array.at[tuple(index_at)].set(smallest)
    longest = shape.index(max(shape))
    index_at[longest] = (index_at[longest] + 1) % shape[longest]
    return array.at[tuple(index_at)].set(largest)


def shard_levels(own_key, shape, cuts, least, top_value):
    level, own = 1.0, jax.random.fold_in(own_key, 6)
    for position, shards_of in cuts:
        draws = jnp.exp(jax.random.uniform(jax.random.fold_in(own, position), (shards_of,), jnp.float32, least / len(cuts), top_value / len(cuts)))
        level = level * jnp.repeat(draws, shape[position] // shards_of).reshape([-1 if axis == position else 1 for axis in range(len(shape))])
    return level


def normal_values(own_key, extent, deviation, reach, shards=(), kind=jnp.bfloat16):
    level = shard_levels(own_key, extent, shards, -0.22, 0.18) if shards else 1.0
    drawn = jax.random.normal(own_key, extent, jnp.float32) * deviation * level
    return jnp.minimum(jnp.maximum(drawn, -reach), reach).astype(kind)


def setup_inputs(seed: int = 0) -> dict:
    key_list = jax.random.split(jax.random.key(seed), 6)
    return {
        "features": normal_values(key_list[0], (TOKENS, 3, D), 1.0, 6.0, ((0, 32),)),
        "cotangent": normal_values(key_list[1], (TOKENS, D), 1.0, 6.0, ((0, 8), (1, 4))),
        "short_filter": normal_values(key_list[2], (3, GROUPS, SHORT), 0.4, 2.5, ((1, 4),), jnp.float32),
        "medium_filter": normal_values(key_list[3], (GROUPS, MEDIUM), MEDIUM ** -0.5, 0.5, ((0, 4),), jnp.float32),
        "doc_start": with_ends(jax.random.randint(key_list[4], (SHARDS,), 0, TOK_DEV), jax.random.fold_in(key_list[4], 1), 0, TOK_DEV - 1).astype(jnp.int32),
    }


ref_block = 128
ref_groups = 32


def doc_ids(doc_start):
    shard_count = doc_start.shape[0]
    bounds = jnp.arange(shard_count, dtype=jnp.int32) * TOK_DEV + doc_start.astype(jnp.int32)
    marks = jnp.zeros((shard_count * TOK_DEV,), jnp.int32).at[bounds].add(1)
    return jnp.cumsum(marks).astype(jnp.int32)


def short_forward(source, chan_taps, doc_index):
    row_count = source.shape[0]
    running = jnp.zeros(source.shape, jnp.float32)
    for offset in range(SHORT):
        shifted = jnp.pad(source[:row_count - offset], ((offset, 0), (0, 0), (0, 0)))
        open_tap = jnp.concatenate([jnp.zeros((offset,), bool), doc_index[:row_count - offset] == doc_index[offset:]])
        running = running + jnp.where(open_tap[:, None, None], chan_taps[None, :, :, offset] * shifted.astype(jnp.float32), 0.0)
    return running


def short_backward(grad_short, chan_taps, doc_index):
    row_count = grad_short.shape[0]
    running = jnp.zeros(grad_short.shape, jnp.float32)
    for offset in range(SHORT):
        shifted = jnp.pad(grad_short[offset:], ((0, offset), (0, 0), (0, 0)))
        open_tap = jnp.concatenate([doc_index[offset:] == doc_index[:row_count - offset], jnp.zeros((offset,), bool)])
        running = running + jnp.where(open_tap[:, None, None], chan_taps[None, :, :, offset] * shifted, 0.0)
    return running


def band_forward(gated, group_filter, doc_index):
    row_count, batch_width = gated.shape
    group_count = group_filter.shape[0]
    group_width = batch_width // group_count
    padded = jnp.concatenate([jnp.zeros((MEDIUM, batch_width), gated.dtype), gated], axis=0)
    padded_ids = jnp.concatenate([jnp.full((MEDIUM,), -1, jnp.int32), doc_index])
    lag_steps = jnp.arange(ref_block, dtype=jnp.int32)[:, None] + MEDIUM - jnp.arange(ref_block + MEDIUM, dtype=jnp.int32)[None, :]
    inside = (lag_steps >= 0) & (lag_steps < MEDIUM)
    lag_table = jnp.where(inside[None], jnp.take(group_filter, jnp.clip(lag_steps, 0, MEDIUM - 1), axis=1), jnp.zeros((), group_filter.dtype))

    def one_block(row_start):
        window = lax.dynamic_slice_in_dim(padded, row_start, ref_block + MEDIUM, 0)
        window_ids = lax.dynamic_slice_in_dim(padded_ids, row_start, ref_block + MEDIUM, 0)
        target_ids = lax.dynamic_slice_in_dim(padded_ids, row_start + MEDIUM, ref_block, 0)
        band_matrix = jnp.where((target_ids[:, None] == window_ids[None, :])[None], lag_table, jnp.zeros((), lag_table.dtype))
        window = window.reshape(ref_block + MEDIUM, group_count, group_width)
        result = jnp.einsum("gts,sgc->tgc", band_matrix.astype(jnp.float32), window.astype(jnp.float32))
        return result.reshape(ref_block, batch_width)

    block_starts = (jnp.arange(row_count // ref_block) * ref_block).astype(jnp.int32)
    return lax.map(one_block, block_starts).reshape(row_count, batch_width)


def band_backward(grad_long, group_filter, doc_index):
    row_count, batch_width = grad_long.shape
    group_count = group_filter.shape[0]
    group_width = batch_width // group_count
    padded = jnp.concatenate([grad_long, jnp.zeros((MEDIUM, batch_width), grad_long.dtype)], axis=0)
    padded_ids = jnp.concatenate([doc_index, jnp.full((MEDIUM,), -1, jnp.int32)])
    lag_steps = jnp.arange(ref_block + MEDIUM, dtype=jnp.int32)[None, :] - jnp.arange(ref_block, dtype=jnp.int32)[:, None]
    inside = (lag_steps >= 0) & (lag_steps < MEDIUM)
    lag_table = jnp.where(inside[None], jnp.take(group_filter, jnp.clip(lag_steps, 0, MEDIUM - 1), axis=1), jnp.zeros((), group_filter.dtype))

    def one_block(row_start):
        window = lax.dynamic_slice_in_dim(padded, row_start, ref_block + MEDIUM, 0)
        window_ids = lax.dynamic_slice_in_dim(padded_ids, row_start, ref_block + MEDIUM, 0)
        target_ids = lax.dynamic_slice_in_dim(padded_ids, row_start, ref_block, 0)
        band_matrix = jnp.where((target_ids[:, None] == window_ids[None, :])[None], lag_table, jnp.zeros((), lag_table.dtype))
        window = window.reshape(ref_block + MEDIUM, group_count, group_width)
        result = jnp.einsum("gts,sgc->tgc", band_matrix.astype(jnp.float32), window.astype(jnp.float32))
        return result.reshape(ref_block, batch_width)

    block_starts = (jnp.arange(row_count // ref_block) * ref_block).astype(jnp.int32)
    return lax.map(one_block, block_starts).reshape(row_count, batch_width)


def reference(features, cotangent, short_filter, medium_filter, doc_start):
    doc_index = doc_ids(doc_start)
    group_width = D // GROUPS
    batch_width = ref_groups * group_width
    row_count = features.shape[0]

    def group_work(batch_index):
        source = lax.dynamic_slice_in_dim(features, batch_index * batch_width, batch_width, 2)
        grad_out = lax.dynamic_slice_in_dim(cotangent, batch_index * batch_width, batch_width, 1)
        batch_taps = lax.dynamic_slice_in_dim(short_filter, batch_index * ref_groups, ref_groups, 1)
        chan_taps = jnp.repeat(batch_taps, group_width, axis=1)
        group_filter = lax.dynamic_slice_in_dim(medium_filter, batch_index * ref_groups, ref_groups, 0).astype(jnp.bfloat16)
        short_out = short_forward(source, chan_taps, doc_index)
        gated = (short_out[:, 1] * short_out[:, 2]).astype(jnp.bfloat16)
        long_conv = band_forward(gated, group_filter, doc_index)
        hyena_out = (short_out[:, 0] * long_conv).astype(jnp.bfloat16)
        grad_query = grad_out.astype(jnp.float32) * long_conv
        grad_long = (grad_out.astype(jnp.float32) * short_out[:, 0]).astype(jnp.bfloat16)
        grad_gated = band_backward(grad_long, group_filter, doc_index)
        grad_short = jnp.stack([grad_query, grad_gated * short_out[:, 2], grad_gated * short_out[:, 1]], axis=1)
        feature_grad = short_backward(grad_short, chan_taps, doc_index).astype(jnp.bfloat16)
        return hyena_out, feature_grad

    outs_all, grads_all = lax.map(group_work, jnp.arange(GROUPS // ref_groups, dtype=jnp.int32))
    hyena_out = jnp.transpose(outs_all, (1, 0, 2)).reshape(row_count, D)
    feature_grad = jnp.transpose(grads_all, (1, 2, 0, 3)).reshape(row_count, 3, D)
    return (hyena_out, feature_grad)
```

```python
import functools

import jax
import jax.numpy as jnp
from jax import lax
from jax.experimental import pallas as pl
from jax.experimental.pallas import tpu as pltpu
from jax.sharding import PartitionSpec as P

SHORT = 7
MEDIUM = 128
EDGE = 8
TAIL = 16
LANES = 128
WIDE = 1024
AHEAD = 2
FAR = 1 << 20
MESH = pl.DeviceIdType.MESH
ANY = pl.BlockSpec(memory_space=pl.ANY)
VMEM = pl.BlockSpec(memory_space=pltpu.VMEM)


def remote(src, dst, ssem, rsem, dev):
    return pltpu.make_async_remote_copy(src, dst, ssem, rsem, device_id=dev, device_id_type=MESH)


def al(i, n):
    return pl.multiple_of(i, n)


def split3(t):
    bf, f32 = jnp.bfloat16, jnp.float32
    high = t.astype(bf)
    rest = t - high.astype(f32)
    mid = rest.astype(bf)
    low = (rest - mid.astype(f32)).astype(bf)
    return high, mid, low


def core_kernel(chans, seqs, span, pieces, x, cot, ctaps, filt, doc, hy, back, bedge, kv, tapsx, fm,
                xk, xprev, xnext, tall, cotv, q, gbuf, gat, gl, kvv, xs, xq, sh, fmq, mf, mb, lf, filtf, filtr, sent,
                hyv,
                esem, fsem, tsem, trsem, lsem, qss, qrs, gss, grs, nsem, hss, hrs, rss, rrs, rls, bss, brs, bls, ksem,
                ysem):
    c, s = lax.axis_index("chan"), lax.axis_index("seq")
    f32, bf = jnp.float32, jnp.bfloat16
    rows = x.shape[1]
    full = x.shape[2]
    more = rows + EDGE
    own, width = cot.shape
    groups = filt.shape[0]
    pw = width // pieces
    tp = pw // LANES
    half = chans // 2
    me = chans - 2
    start = s * own

    bar = pltpu.get_barrier_semaphore()
    for k in range(1, chans):
        pl.semaphore_signal(bar, inc=1, device_id={"chan": lax.rem(c + k, chans)}, device_id_type=MESH)
    for step in (1, seqs - 1):
        for k in range(chans):
            dev = {"seq": lax.rem(s + step, seqs), "chan": lax.rem(c + k, chans)}
            pl.semaphore_signal(bar, inc=1, device_id=dev, device_id_type=MESH)
    up, down = {"seq": lax.rem(s + 1, seqs)}, {"seq": lax.rem(s + seqs - 1, seqs)}
    after = {"seq": lax.rem(s + (c + 1) // chans, seqs), "chan": lax.rem(c + 1, chans)}
    ahead = {"seq": lax.rem(s + seqs - 1 + (c + chans - 1) // chans, seqs), "chan": lax.rem(c + chans - 1, chans)}

    def owner(k):
        return lax.rem(c // 2 + 1 + k // 2, half) * 2 + lax.rem(lax.rem(c, 2) + lax.rem(k, 2), 2)

    mine = pl.ds(al(TAIL + c * rows, 16), rows)
    gmine = pl.ds(al(MEDIUM + c * rows, 16), rows)

    def cols(d, p):
        return pl.ds(al(d * width + p * pw, LANES), pw)

    def part(p):
        return pl.ds(al(p * pw, LANES), pw)

    def q_send(p, k):
        d = owner(k)
        far = remote(x.at[0, :, cols(d, p)], q.at[mine, part(p)], qss.at[p, k], qrs.at[p, k], {"chan": d})
        near = pltpu.make_async_copy(x.at[0, :, cols(d, p)], q.at[mine, part(p)], qrs.at[p, k])
        return far, near

    def g_send(p, k):
        d = owner(k)
        far = remote(gbuf.at[:, cols(d, p)], gat.at[gmine, part(p)], gss.at[p, k], grs.at[p, k], {"chan": d})
        near = pltpu.make_async_copy(gbuf.at[:, cols(d, p)], gat.at[gmine, part(p)], grs.at[p, k])
        return far, near

    def kv_keep(p, k):
        at = cols(owner(k), p)
        return pltpu.make_async_copy(kvv.at[:, :, at], kv.at[:, :, at], ksem.at[p, k])

    def q_up(p):
        return remote(q.at[pl.ds(own, TAIL), part(p)], q.at[pl.ds(0, TAIL), part(p)], hss.at[0, p], hrs.at[0, p], up)

    def g_up(p):
        return remote(gat.at[pl.ds(own, MEDIUM), part(p)], gat.at[pl.ds(0, MEDIUM), part(p)], hss.at[1, p],
                      hrs.at[1, p], up)

    def l_down(p):
        return remote(gl.at[pl.ds(0, MEDIUM), part(p)], gl.at[pl.ds(own, MEDIUM), part(p)], hss.at[2, p],
                      hrs.at[2, p], down)

    def r_send(t, k):
        d = owner(k)
        at = pl.ds(al(t * LANES, LANES), LANES)
        to = pl.ds(al(c * width + t * LANES, LANES), LANES)
        src = sent.at[:, pl.ds(al(d * rows, 16), rows), at]
        if k == me:
            return pltpu.make_async_copy(src, back.at[:, :, to], rls.at[t])
        return remote(src, back.at[:, :, to], rss.at[t, k], rrs.at[t, k], {"chan": d})

    def e_send(p, k):
        d = owner(k)
        at = part(p)
        to = cols(c, p)
        if k == me:
            return pltpu.make_async_copy(
                sent.at[:, pl.ds(al(lax.rem(c + 1, chans) * rows, 16), EDGE), at], bedge.at[:, :, to], bls.at[p])
        first = lax.rem(d + 1, chans)
        back_one = (d + 1) // chans
        dev = {"seq": lax.rem(s + seqs - back_one, seqs), "chan": d}
        return remote(sent.at[:, pl.ds(al(first * rows, 16), EDGE), at], bedge.at[:, :, to], bss.at[p, k],
                      brs.at[p, k], dev)

    def e_wrap(p):
        dev = {"seq": lax.rem(s + seqs - 1, seqs), "chan": c}
        return remote(sent.at[:, pl.ds(0, EDGE), part(p)], bedge.at[:, :, cols(c, p)], bss.at[p, me], brs.at[p, me],
                      dev)

    loads = [
        pltpu.make_async_copy(x.at[pl.ds(1, 2)], xk, lsem.at[0]),
        pltpu.make_async_copy(cot, cotv, lsem.at[1]),
        pltpu.make_async_copy(ctaps, tall.at[c], lsem.at[2]),
    ]
    for cp in loads:
        cp.start()

    low = jnp.maximum(s - 1, 0)
    high = jnp.minimum(s + 1, seqs - 1)
    b0 = (s - 1) * own + doc[low]
    b1 = s * own + doc[s]
    b2 = (s + 1) * own + doc[high]
    tokens = seqs * own

    def ids(pos):
        one = lambda b: jnp.where(pos >= b, 1, 0)
        seg = one(b0) + one(b1) + one(b2)
        return jnp.where(pos < 0, -1, jnp.where(pos >= tokens, FAR, seg))

    pl.semaphore_wait(bar, chans - 1 + 2 * chans)
    early = [
        remote(x.at[pl.ds(1, 2), pl.ds(rows - EDGE, EDGE)], xprev, esem.at[0], fsem.at[0], after),
        remote(x.at[pl.ds(1, 2), pl.ds(0, EDGE)], xnext, esem.at[1], fsem.at[1], ahead),
    ]
    for k in range(chans):
        if k != me:
            early.append(remote(ctaps, tall.at[c], tsem.at[k], trsem.at[k], {"chan": owner(k)}))
    for cp in early:
        cp.start()
    for p in range(min(AHEAD, pieces)):
        for k in range(chans):
            q_send(p, k)[1 if k == me else 0].start()

    pos = start + c * rows + lax.broadcasted_iota(jnp.int32, (more, LANES), 0)
    here = ids(pos)
    for j in range(1, SHORT):
        fm[j - 1] = jnp.where(here == ids(pos - j), 1.0, 0.0)
    pos = start + lax.broadcasted_iota(jnp.int32, (own, LANES), 0)
    here = ids(pos)
    for j in range(1, SHORT):
        fmq[j - 1] = jnp.where(here == ids(pos - j), 1.0, 0.0)
    r = lax.broadcasted_iota(jnp.int32, (MEDIUM, 2 * MEDIUM), 0)
    k2 = lax.broadcasted_iota(jnp.int32, (MEDIUM, 2 * MEDIUM), 1)
    for b in range(own // MEDIUM):
        base = start + b * MEDIUM
        here = ids(base + r)
        lag = r + MEDIUM - k2
        ok = (lag >= 0) & (lag < MEDIUM) & (here == ids(base - MEDIUM + k2))
        mf[b] = jnp.where(ok, 1.0, 0.0).astype(bf)
        lag = k2 - r
        ok = (lag >= 0) & (lag < MEDIUM) & (here == ids(base + k2))
        mb[b] = jnp.where(ok, 1.0, 0.0).astype(bf)
    rounded = filt[...].astype(bf)
    filtf[...] = rounded.astype(f32)
    ri = lax.broadcasted_iota(jnp.int32, (MEDIUM, MEDIUM), 0)
    ci = lax.broadcasted_iota(jnp.int32, (MEDIUM, MEDIUM), 1)
    turn = jnp.where(lax.rem(ri + ci, MEDIUM) == 0, 1.0, 0.0).astype(bf)
    filtr[...] = jnp.dot(rounded, turn, preferred_element_type=f32)

    for cp in loads:
        cp.wait()
    for cp in early:
        cp.wait()

    def widen(n, carry):
        at = n * pw
        row = lax.broadcasted_iota(jnp.int32, (groups, pw), 0)
        col = lax.broadcasted_iota(jnp.int32, (groups, pw), 1)
        hot = jnp.where(row == (at + col) // span, 1.0, 0.0).astype(bf)
        for d in range(chans):
            full_taps = tall[d].reshape(24, groups)
            high, mid, low3 = (jnp.dot(v, hot, preferred_element_type=f32) for v in split3(full_taps))
            tapsx[d, :, pl.ds(al(at, LANES), pw)] = high + (mid + low3)
        return carry

    lax.fori_loop(0, pieces, widen, 0)

    def chunk(n, carry):
        p, k = n // chans, lax.rem(n, chans)
        d = owner(k)

        for t in range(tp):
            lane = pl.ds(al(p * pw + t * LANES, LANES), LANES)
            at = pl.ds(al(d * width + p * pw + t * LANES, LANES), LANES)
            outs = []
            for m in range(2):
                z = 2 * (t % 2) + m
                xs[z, pl.ds(0, EDGE), :] = xprev[m, :, at].astype(f32)
                xs[z, pl.ds(EDGE, rows), :] = xk[m, :, at].astype(f32)
                xs[z, pl.ds(EDGE + rows, EDGE), :] = xnext[m, :, at].astype(f32)
                tap = lambda j: tapsx[d, 8 * (m + 1) + j : 8 * (m + 1) + j + 1, lane]
                total = tap(0) * xs[z, pl.ds(EDGE, more), :]
                for j in range(1, SHORT):
                    total = total + tap(j) * (fm[j - 1] * xs[z, pl.ds(EDGE - j, more), :])
                kvv[m, :, at] = total
                outs.append(total[:rows])
            gbuf[:, at] = (outs[0] * outs[1]).astype(bf)

        kv_keep(p, k).start()
        far, near = g_send(p, k)

        @pl.when((p < AHEAD) & (k == me))
        def _():
            near.start()

        @pl.when((p < AHEAD) & (k != me))
        def _():
            far.start()

        return carry

    lax.fori_loop(0, pieces * chans, chunk, 0)

    lane_group = lax.broadcasted_iota(jnp.int32, (MEDIUM, LANES), 1) // span
    per = LANES // span
    blocks = own // MEDIUM

    def query(t, carry):
        at = pl.ds(al(t * LANES, LANES), LANES)
        xq[...] = q[:, at].astype(f32)
        step = 64
        for lo in range(0, own, step):
            tap = lambda j: tapsx[c, j : j + 1, at]
            total = tap(0) * xq[pl.ds(TAIL + lo, step), :]
            for j in range(1, SHORT):
                total = total + tap(j) * (fmq[j - 1, pl.ds(lo, step), :] * xq[pl.ds(TAIL + lo - j, step), :])
            sh[pl.ds(lo, step), at] = total
            gl[pl.ds(lo, step), at] = (cotv[pl.ds(lo, step), at].astype(f32) * total).astype(bf)
        return carry

    def mix(t, carry):
        at = pl.ds(al(t * LANES, LANES), LANES)
        rowset = pl.ds(al(t * per, per), per)

        def band(filters, masks):
            for g in range(per):
                row = jnp.broadcast_to(filters[g : g + 1, :], (MEDIUM, MEDIUM))
                circ = pltpu.roll(row, 0, 1, stride=1, stride_axis=0).astype(bf)
                two = jnp.concatenate([circ, circ], axis=1)
                for b in range(blocks):
                    lf[b, pl.ds(g * MEDIUM, MEDIUM), :] = two * masks[b]

        def product(b, source):
            rhs = source[pl.ds(MEDIUM * b, 2 * MEDIUM), at]
            res = jnp.dot(lf[b], rhs, preferred_element_type=f32)
            total = res[:MEDIUM]
            for g in range(1, per):
                total = jnp.where(lane_group == g, res[g * MEDIUM : (g + 1) * MEDIUM], total)
            return total

        band(filtr[rowset, :], mf)
        for b in range(blocks):
            long = product(b, gat)
            lo = pl.ds(MEDIUM * b, MEDIUM)
            hyv[lo, at] = (sh[lo, at] * long).astype(bf)
            sent[0, lo, at] = (cotv[lo, at].astype(f32) * long).astype(bf)
        band(filtf[rowset, :], mb)
        for b in range(blocks):
            sent[1, pl.ds(MEDIUM * b, MEDIUM), at] = product(b, gl).astype(bf)
        for k in range(chans):
            r_send(t, k).start()
        return carry

    def edges(p):
        return [e_send(p, k) for k in range(chans) if k != me]

    def hy_keep(p):
        return pltpu.make_async_copy(hyv.at[:, part(p)], hy.at[:, part(p)], ysem.at[p])

    def stage(p, carry):
        @pl.when(p < pieces)
        def _():
            for k in range(chans):
                q_send(p, k)[1 if k == me else 0].wait() if k == me else q_send(p, k)[0].wait_recv()
            q_up(p).start()
            for k in range(chans):
                g_send(p, k)[1].wait() if k == me else g_send(p, k)[0].wait_recv()
            g_up(p).start()

        @pl.when(p + AHEAD < pieces)
        def _():
            for k in range(chans):
                q_send(p + AHEAD, k)[1 if k == me else 0].start()
            for k in range(chans):
                g_send(p + AHEAD, k)[1 if k == me else 0].start()

        @pl.when(p > 0)
        def _():
            g_up(p - 1).wait()
            l_down(p - 1).wait()
            lax.fori_loop((p - 1) * tp, p * tp, mix, 0)
            hy_keep(p - 1).start()
            for cp in edges(p - 1):
                cp.start()

            @pl.when(c == chans - 1)
            def _():
                e_wrap(p - 1).start()

            @pl.when(c < chans - 1)
            def _():
                e_send(p - 1, me).start()

        @pl.when(p < pieces)
        def _():
            q_up(p).wait()
            lax.fori_loop(p * tp, (p + 1) * tp, query, 0)
            l_down(p).start()

        return carry

    lax.fori_loop(0, pieces + 1, stage, 0)

    def finish(p, carry):
        for k in range(chans):
            if k != me:
                q_send(p, k)[0].wait_send()
                g_send(p, k)[0].wait_send()
            kv_keep(p, k).wait()
        for cp in edges(p):
            cp.wait()

        @pl.when(c == chans - 1)
        def _():
            e_wrap(p).wait()

        @pl.when(c < chans - 1)
        def _():
            e_send(p, me).wait()

        hy_keep(p).wait()
        return carry

    lax.fori_loop(0, pieces, finish, 0)

    def leave(t, carry):
        for k in range(chans):
            r_send(t, k).wait()
        return carry

    lax.fori_loop(0, pieces * tp, leave, 0)


def last_kernel(g, ge, kv, tapsx, fm, hy, out, hy_out, gs, sem):
    rows = out.shape[1]
    more = rows + EDGE
    f32 = jnp.float32
    copy = pltpu.make_async_copy(hy, hy_out, sem)

    @pl.when(pl.program_id(0) == 0)
    def _():
        copy.start()

    for t in range(out.shape[2] // LANES):
        at = pl.ds(t * LANES, LANES)
        for m in range(3):
            z = 3 * (t % 2) + m
            top = g[min(m, 1), :, at].astype(f32)
            end = ge[min(m, 1), :, at].astype(f32)
            if m:
                top = top * kv[2 - m, pl.ds(0, rows), at]
                end = end * kv[2 - m, pl.ds(rows, EDGE), at]
            gs[z, pl.ds(0, rows), :] = top
            gs[z, pl.ds(rows, EDGE), :] = end
            tap = lambda j: tapsx[8 * m + j : 8 * m + j + 1, at]
            total = tap(0) * gs[z, pl.ds(0, rows), :]
            for j in range(1, SHORT):
                total = total + tap(j) * (fm[j - 1, pl.ds(j, rows), :] * gs[z, pl.ds(j, rows), :])
            out[m, :, at] = total.astype(jnp.bfloat16)

    @pl.when(pl.program_id(0) == pl.num_programs(0) - 1)
    def _():
        copy.wait()


def solution(mesh):
    chans, seqs = mesh.shape["chan"], mesh.shape["seq"]

    def body(features, cotangent, short_filter, medium_filter, doc_start):
        own, width = cotangent.shape
        rows, _, full = features.shape
        groups = medium_filter.shape[0]
        span = full // (groups * chans)
        more = rows + EDGE
        bf, f32 = jnp.bfloat16, jnp.float32
        shape = jax.ShapeDtypeStruct
        dma = lambda *dims: pltpu.SemaphoreType.DMA(dims)
        x = jnp.transpose(features, (1, 0, 2))
        ctaps = jnp.pad(jnp.transpose(short_filter, (0, 2, 1)), ((0, 0), (0, 1), (0, 0)))
        limit = 60 << 20
        tiles = width // LANES
        pieces = min(4, tiles)
        wide = min(WIDE, width)
        blocks = own // MEDIUM
        per = LANES // span
        vm = pltpu.VMEM

        hy, back, bedge, kv, tapsx, fm = pl.pallas_call(
            functools.partial(core_kernel, chans, seqs, span, pieces),
            out_shape=(
                shape((own, width), bf), shape((2, rows, full), bf), shape((2, EDGE, full), bf),
                shape((2, more, full), f32), shape((chans, 24, width), f32), shape((SHORT - 1, more, LANES), f32)),
            in_specs=[ANY, ANY, ANY, VMEM, pl.BlockSpec(memory_space=pltpu.SMEM)],
            out_specs=(ANY, ANY, ANY, ANY, VMEM, VMEM),
            scratch_shapes=[
                vm((2, rows, full), bf), vm((2, EDGE, full), bf), vm((2, EDGE, full), bf),
                vm((chans, 3, 8, groups), f32), vm((own, width), bf), vm((TAIL + own, width), bf),
                vm((rows, full), bf), vm((MEDIUM + own, width), bf), vm((own + MEDIUM, width), bf),
                vm((2, more, full), f32), vm((4, rows + 2 * EDGE, LANES), f32), vm((TAIL + own, LANES), f32),
                vm((own, width), f32), vm((SHORT - 1, own, LANES), f32),
                vm((blocks, MEDIUM, 2 * MEDIUM), bf), vm((blocks, MEDIUM, 2 * MEDIUM), bf),
                vm((blocks, per * MEDIUM, 2 * MEDIUM), bf), vm((groups, MEDIUM), f32), vm((groups, MEDIUM), f32),
                vm((2, own, width), bf), vm((own, width), bf),
                dma(2), dma(2), dma(chans), dma(chans), dma(3),
                dma(pieces, chans), dma(pieces, chans), dma(pieces, chans), dma(pieces, chans), dma(1),
                dma(3, pieces), dma(3, pieces), dma(tiles, chans), dma(tiles, chans), dma(tiles),
                dma(pieces, chans), dma(pieces, chans), dma(pieces), dma(pieces, chans), dma(pieces),
            ],
            compiler_params=pltpu.CompilerParams(
                collective_id=0, has_side_effects=True, vmem_limit_bytes=limit),
            name="core",
        )(x, cotangent, ctaps, medium_filter, doc_start)

        per_owner = width // wide
        cube = lambda m, n: pl.BlockSpec((m, n, wide), lambda i: (0, 0, i))
        grad, hy = pl.pallas_call(
            last_kernel,
            grid=(full // wide,),
            out_shape=(shape((3, rows, full), bf), shape((own, width), bf)),
            in_specs=[
                cube(2, rows), cube(2, EDGE), cube(2, more),
                pl.BlockSpec((None, 24, wide), lambda i: (i // per_owner, 0, i % per_owner)),
                pl.BlockSpec(fm.shape, lambda i: (0, 0, 0)), ANY,
            ],
            out_specs=(cube(3, rows), ANY),
            scratch_shapes=[vm((6, more, LANES), f32), pltpu.SemaphoreType.DMA],
            compiler_params=pltpu.CompilerParams(vmem_limit_bytes=limit),
            name="last_rows",
        )(back, bedge, kv, tapsx, fm, hy)
        return hy, jnp.transpose(grad, (1, 0, 2))

    in_specs = (
        P(("seq", "chan"), None, None),
        P("seq", "chan"),
        P(None, "chan", None),
        P("chan", None),
        P(),
    )
    out_specs = (P("seq", "chan"), P(("seq", "chan"), None, None))
    return jax.shard_map(body, mesh=mesh, in_specs=in_specs, out_specs=out_specs, check_vma=False)
```

```python
import functools

import jax
import jax.numpy as jnp
from jax import lax
from jax.experimental import pallas as pl
from jax.experimental.pallas import tpu as pltpu
from jax.sharding import PartitionSpec as P

SHORT = 7
MEDIUM = 128
EDGE = 8
TAIL = 16
LANES = 128
WIDE = 2048
PIECES = 8
AHEAD = 3
SKEW = 3
HOLD = 2
FAR = 1 << 20
MESH = pl.DeviceIdType.MESH
ANY = pl.BlockSpec(memory_space=pl.ANY)
VMEM = pl.BlockSpec(memory_space=pltpu.VMEM)


def remote(src, dst, ssem, rsem, dev):
    return pltpu.make_async_remote_copy(src, dst, ssem, rsem, device_id=dev, device_id_type=MESH)


def al(i, n):
    return pl.multiple_of(i, n)


def split3(t):
    bf, f32 = jnp.bfloat16, jnp.float32
    high = t.astype(bf)
    rest = t - high.astype(f32)
    mid = rest.astype(bf)
    low = (rest - mid.astype(f32)).astype(bf)
    return high, mid, low


def core_kernel(chans, seqs, span, pieces, x, cot, ctaps, filt, doc, hy, fq, back, bedge, kv, kvx, tapsx, fm,
                xk, xprev, xnext, tall, cotv, q, gbuf, gat, gl, kvv, kvxv, xs, xe, xq, sh, fmq, mf, mb, lf, filtf, filtr, sent, gq,
                hyv,
                esem, fsem, tsem, trsem, lsem, qss, qrs, gss, grs, nsem, hss, hrs, rss, rrs, rls, bss, brs, bls, ksem,
                ysem):
    c, s = lax.axis_index("chan"), lax.axis_index("seq")
    f32, bf = jnp.float32, jnp.bfloat16
    rows = x.shape[1]
    full = x.shape[2]
    more = rows + EDGE
    own, width = cot.shape
    groups = filt.shape[0]
    pw = width // pieces
    tp = pw // LANES
    half = chans // 2
    me = chans - 2
    start = s * own

    bar = pltpu.get_barrier_semaphore()
    for k in range(1, chans):
        pl.semaphore_signal(bar, inc=1, device_id={"chan": lax.rem(c + k, chans)}, device_id_type=MESH)
    for step in (1, seqs - 1):
        for k in range(chans):
            dev = {"seq": lax.rem(s + step, seqs), "chan": lax.rem(c + k, chans)}
            pl.semaphore_signal(bar, inc=1, device_id=dev, device_id_type=MESH)
    up, down = {"seq": lax.rem(s + 1, seqs)}, {"seq": lax.rem(s + seqs - 1, seqs)}
    after = {"seq": lax.rem(s + (c + 1) // chans, seqs), "chan": lax.rem(c + 1, chans)}
    ahead = {"seq": lax.rem(s + seqs - 1 + (c + chans - 1) // chans, seqs), "chan": lax.rem(c + chans - 1, chans)}

    def owner(k):
        return lax.rem(c // 2 + 1 + k // 2, half) * 2 + lax.rem(lax.rem(c, 2) + lax.rem(k, 2), 2)

    mine = pl.ds(al(TAIL + c * rows, 16), rows)
    gmine = pl.ds(al(MEDIUM + c * rows, 16), rows)

    def cols(d, p):
        return pl.ds(al(d * width + p * pw, LANES), pw)

    def part(p):
        return pl.ds(al(p * pw, LANES), pw)

    def q_send(p, k):
        d = owner(k)
        if k == me:
            return pltpu.make_async_copy(x.at[0, :, cols(d, p)], q.at[mine, part(p)], qrs.at[p, k])
        return remote(x.at[0, :, cols(d, p)], q.at[mine, part(p)], qss.at[p, k], qrs.at[p, k], {"chan": d})

    def g_send(p, k):
        d = owner(k)
        if k == me:
            return pltpu.make_async_copy(gbuf.at[:, cols(d, p)], gat.at[gmine, part(p)], grs.at[p, k])
        return remote(gbuf.at[:, cols(d, p)], gat.at[gmine, part(p)], gss.at[p, k], grs.at[p, k], {"chan": d})

    def kv_keep(p, k):
        at = cols(owner(k), p)
        return pltpu.make_async_copy(kvv.at[:, :, at], kv.at[:, :, at], ksem.at[p, k])

    def q_up(p):
        return remote(q.at[pl.ds(own, TAIL), part(p)], q.at[pl.ds(0, TAIL), part(p)], hss.at[0, p], hrs.at[0, p], up)

    def g_up(p):
        return remote(gat.at[pl.ds(own, MEDIUM), part(p)], gat.at[pl.ds(0, MEDIUM), part(p)], hss.at[1, p],
                      hrs.at[1, p], up)

    def l_down(p):
        return remote(gl.at[pl.ds(0, MEDIUM), part(p)], gl.at[pl.ds(own, MEDIUM), part(p)], hss.at[2, p],
                      hrs.at[2, p], down)

    def gq_down(p):
        return remote(gq.at[pl.ds(0, EDGE), part(p)], gq.at[pl.ds(own, EDGE), part(p)], hss.at[3, p], hrs.at[3, p],
                      down)

    def r_send(m, p, k):
        d = owner(k)
        src = sent.at[m, pl.ds(al(d * rows, 16), rows), part(p)]
        dst = (fq, back)[m].at[:, cols(c, p)]
        if k == me:
            return pltpu.make_async_copy(src, dst, rls.at[m, p])
        return remote(src, dst, rss.at[m, p, k], rrs.at[m, p, k], {"chan": d})

    def e_send(p, k):
        d = owner(k)
        src = sent.at[1, pl.ds(al(lax.rem(d + 1, chans) * rows, 16), EDGE), part(p)]
        dst = bedge.at[:, cols(c, p)]
        if k == me:
            return pltpu.make_async_copy(src, dst, bls.at[p])
        dev = {"seq": lax.rem(s + seqs - (d + 1) // chans, seqs), "chan": d}
        return remote(src, dst, bss.at[p, k], brs.at[p, k], dev)

    def e_wrap(p):
        dev = {"seq": lax.rem(s + seqs - 1, seqs), "chan": c}
        return remote(sent.at[1, pl.ds(0, EDGE), part(p)], bedge.at[:, cols(c, p)], bss.at[p, me], brs.at[p, me], dev)

    loads = [
        pltpu.make_async_copy(x.at[pl.ds(1, 2)], xk, lsem.at[0]),
        pltpu.make_async_copy(cot, cotv, lsem.at[1]),
    ]
    for cp in loads:
        cp.start()

    tall[c] = jnp.zeros(tall.shape[1:], f32)
    tall[c, :, pl.ds(0, SHORT), :] = ctaps[...]

    low = jnp.maximum(s - 1, 0)
    high = jnp.minimum(s + 1, seqs - 1)
    b0 = (s - 1) * own + doc[low]
    b1 = s * own + doc[s]
    b2 = (s + 1) * own + doc[high]
    tokens = seqs * own

    def ids(pos):
        one = lambda b: jnp.where(pos >= b, 1, 0)
        seg = one(b0) + one(b1) + one(b2)
        return jnp.where(pos < 0, -1, jnp.where(pos >= tokens, FAR, seg))

    pl.semaphore_wait(bar, chans - 1 + 2 * chans)
    taps = []
    early = [
        remote(x.at[pl.ds(1, 2), pl.ds(rows - EDGE, EDGE)], xprev, esem.at[0], fsem.at[0], after),
    ]
    later = remote(x.at[pl.ds(1, 2), pl.ds(0, EDGE)], xnext, esem.at[1], fsem.at[1], ahead)
    for k in range(chans):
        if k != me:
            taps.append(remote(tall.at[c], tall.at[c], tsem.at[k], trsem.at[k], {"chan": owner(k)}))
    for cp in early + taps:
        cp.start()

    pos = start + c * rows + lax.broadcasted_iota(jnp.int32, (more, LANES), 0)
    here = ids(pos)
    for j in range(1, SHORT):
        fm[j - 1] = jnp.where(here == ids(pos - j), 1.0, 0.0)
    for p in range(min(AHEAD, pieces)):
        for k in range(chans):
            q_send(p, k).start()
    pos = start + lax.broadcasted_iota(jnp.int32, (own + EDGE, LANES), 0)
    here = ids(pos)
    for j in range(1, SHORT):
        fmq[j - 1] = jnp.where(here == ids(pos - j), 1.0, 0.0)
    r = lax.broadcasted_iota(jnp.int32, (MEDIUM, 2 * MEDIUM), 0)
    k2 = lax.broadcasted_iota(jnp.int32, (MEDIUM, 2 * MEDIUM), 1)
    for b in range(own // MEDIUM):
        base = start + b * MEDIUM
        here = ids(base + r)
        lag = r + MEDIUM - k2
        ok = (lag >= 0) & (lag < MEDIUM) & (here == ids(base - MEDIUM + k2))
        mf[b] = jnp.where(ok, 1.0, 0.0).astype(bf)
        lag = k2 - r
        ok = (lag >= 0) & (lag < MEDIUM) & (here == ids(base + k2))
        mb[b] = jnp.where(ok, 1.0, 0.0).astype(bf)
    rounded = filt[...].astype(bf)
    filtf[...] = rounded.astype(f32)
    ri = lax.broadcasted_iota(jnp.int32, (MEDIUM, MEDIUM), 0)
    ci = lax.broadcasted_iota(jnp.int32, (MEDIUM, MEDIUM), 1)
    turn = jnp.where(lax.rem(ri + ci, MEDIUM) == 0, 1.0, 0.0).astype(bf)
    filtr[...] = jnp.dot(rounded, turn, preferred_element_type=f32)

    for cp in taps:
        cp.wait()

    def widen(n, carry):
        at = n * pw
        row = lax.broadcasted_iota(jnp.int32, (groups, pw), 0)
        col = lax.broadcasted_iota(jnp.int32, (groups, pw), 1)
        hot = jnp.where(row == (at + col) // span, 1.0, 0.0).astype(bf)
        for d in range(chans):
            full_taps = tall[d].reshape(24, groups)
            high, mid, low3 = (jnp.dot(v, hot, preferred_element_type=f32) for v in split3(full_taps))
            tapsx[d, :, pl.ds(al(at, LANES), pw)] = high + (mid + low3)
        return carry

    lax.fori_loop(0, pieces, widen, 0)
    for cp in loads + early:
        cp.wait()

    def chunk(n, carry):
        p, k = n // chans, lax.rem(n, chans)
        d = owner(k)
        for t in range(tp):
            lane = pl.ds(al(p * pw + t * LANES, LANES), LANES)
            at = pl.ds(al(d * width + p * pw + t * LANES, LANES), LANES)
            outs = []
            for m in range(2):
                z = 2 * (t % 2) + m
                xs[z, pl.ds(0, EDGE), :] = xprev[m, :, at].astype(f32)
                xs[z, pl.ds(EDGE, rows), :] = xk[m, :, at].astype(f32)
                tap = lambda j: tapsx[d, 8 * (m + 1) + j : 8 * (m + 1) + j + 1, lane]
                total = tap(0) * xs[z, pl.ds(EDGE, rows), :]
                for j in range(1, SHORT):
                    total = total + tap(j) * (fm[j - 1, pl.ds(0, rows), :] * xs[z, pl.ds(EDGE - j, rows), :])
                kvv[m, :, at] = total
                outs.append(total)
            gbuf[:, at] = (outs[0] * outs[1]).astype(bf)
        kv_keep(p, k).start()
        return carry

    def rowside(p, carry):
        lax.fori_loop(p * chans, (p + 1) * chans, chunk, 0)

        @pl.when(p < AHEAD)
        def _():
            for k in range(chans):
                g_send(p, k).start()

        return carry

    lax.fori_loop(0, pieces, rowside, 0)
    later.start()

    def beyond(n, carry):
        d, at0 = n // (pieces * tp), lax.rem(n, pieces * tp)
        lane = pl.ds(al(at0 * LANES, LANES), LANES)
        at = pl.ds(al(n * LANES, LANES), LANES)
        for m in range(2):
            xe[m, pl.ds(0, EDGE), :] = xk[m, pl.ds(rows - EDGE, EDGE), at].astype(f32)
            xe[m, pl.ds(EDGE, EDGE), :] = xnext[m, :, at].astype(f32)
            tap = lambda j: tapsx[d, 8 * (m + 1) + j : 8 * (m + 1) + j + 1, lane]
            total = tap(0) * xe[m, pl.ds(EDGE, EDGE), :]
            for j in range(1, SHORT):
                total = total + tap(j) * (fm[j - 1, pl.ds(rows, EDGE), :] * xe[m, pl.ds(EDGE - j, EDGE), :])
            kvxv[m, :, at] = total
        return carry

    lane_group = lax.broadcasted_iota(jnp.int32, (MEDIUM, LANES), 1) // span
    per = LANES // span
    blocks = own // MEDIUM

    def query(t, carry):
        at = pl.ds(al(t * LANES, LANES), LANES)
        xq[...] = q[:, at].astype(f32)
        step = 64
        for lo in range(0, own, step):
            tap = lambda j: tapsx[c, j : j + 1, at]
            total = tap(0) * xq[pl.ds(TAIL + lo, step), :]
            for j in range(1, SHORT):
                total = total + tap(j) * (fmq[j - 1, pl.ds(lo, step), :] * xq[pl.ds(TAIL + lo - j, step), :])
            sh[pl.ds(lo, step), at] = total
            gl[pl.ds(lo, step), at] = (cotv[pl.ds(lo, step), at].astype(f32) * total).astype(bf)
        return carry

    def band(filters, masks):
        for g in range(per):
            row = jnp.broadcast_to(filters[g : g + 1, :], (MEDIUM, MEDIUM))
            circ = pltpu.roll(row, 0, 1, stride=1, stride_axis=0).astype(bf)
            two = jnp.concatenate([circ, circ], axis=1)
            for b in range(blocks):
                lf[b, pl.ds(g * MEDIUM, MEDIUM), :] = two * masks[b]

    def product(b, source, at):
        rhs = source[pl.ds(MEDIUM * b, 2 * MEDIUM), at]
        res = jnp.dot(lf[b], rhs, preferred_element_type=f32)
        total = res[:MEDIUM]
        for g in range(1, per):
            total = jnp.where(lane_group == g, res[g * MEDIUM : (g + 1) * MEDIUM], total)
        return total

    def forward(t, carry):
        at = pl.ds(al(t * LANES, LANES), LANES)
        band(filtr[pl.ds(al(t * per, per), per), :], mf)
        for b in range(blocks):
            long = product(b, gat, at)
            lo = pl.ds(MEDIUM * b, MEDIUM)
            hyv[lo, at] = (sh[lo, at] * long).astype(bf)
            gq[lo, at] = cotv[lo, at].astype(f32) * long
        return carry

    def backward(t, carry):
        at = pl.ds(al(t * LANES, LANES), LANES)
        band(filtf[pl.ds(al(t * per, per), per), :], mb)
        for b in range(blocks):
            sent[1, pl.ds(MEDIUM * b, MEDIUM), at] = product(b, gl, at).astype(bf)
        return carry

    def query_back(t, carry):
        at = pl.ds(al(t * LANES, LANES), LANES)
        xq[pl.ds(0, own + EDGE), :] = gq[:, at]
        step = 64
        for lo in range(0, own, step):
            tap = lambda j: tapsx[c, j : j + 1, at]
            total = tap(0) * xq[pl.ds(lo, step), :]
            for j in range(1, SHORT):
                total = total + tap(j) * (fmq[j - 1, pl.ds(lo + j, step), :] * xq[pl.ds(lo + j, step), :])
            sent[0, pl.ds(lo, step), at] = total.astype(bf)
        return carry

    def edges(p):
        return [e_send(p, k) for k in range(chans) if k != me]

    def hy_keep(p):
        return pltpu.make_async_copy(hyv.at[:, part(p)], hy.at[:, part(p)], ysem.at[p])

    def give(p, carry):
        for k in range(chans):
            r_send(1, p, k).start()
        for cp in edges(p):
            cp.start()

        @pl.when(c == chans - 1)
        def _():
            e_wrap(p).start()

        @pl.when(c < chans - 1)
        def _():
            e_send(p, me).start()

        for k in range(chans):
            r_send(0, p, k).start()
        return carry

    hold = max(SKEW, pieces - HOLD)

    def stage(p, carry):
        @pl.when(p < pieces)
        def _():
            for k in range(chans):
                q_send(p, k).wait() if k == me else q_send(p, k).wait_recv()
            q_up(p).start()
            for k in range(chans):
                g_send(p, k).wait() if k == me else g_send(p, k).wait_recv()
            g_up(p).start()

        @pl.when(p + AHEAD < pieces)
        def _():
            for k in range(chans):
                q_send(p + AHEAD, k).start()
            for k in range(chans):
                g_send(p + AHEAD, k).start()

        @pl.when(p == hold)
        def _():
            lax.fori_loop(0, hold - SKEW, give, 0)

        @pl.when((p > 0) & (p <= pieces))
        def _():
            q_up(p - 1).wait()
            lax.fori_loop((p - 1) * tp, p * tp, query, 0)
            l_down(p - 1).start()

        @pl.when((p >= SKEW - 1) & (p < pieces + SKEW - 1))
        def _():
            f = p - SKEW + 1
            g_up(f).wait()
            lax.fori_loop(f * tp, (f + 1) * tp, forward, 0)
            gq_down(f).start()
            hy_keep(f).start()

        @pl.when(p >= SKEW)
        def _():
            f = p - SKEW
            l_down(f).wait()
            lax.fori_loop(f * tp, (f + 1) * tp, backward, 0)
            gq_down(f).wait()
            lax.fori_loop(f * tp, (f + 1) * tp, query_back, 0)

            @pl.when(p >= hold)
            def _():
                give(f, 0)

        return carry

    lax.fori_loop(0, pieces + SKEW, stage, 0)
    later.wait()
    lax.fori_loop(0, chans * pieces * tp, beyond, 0)
    keep = pltpu.make_async_copy(kvxv, kvx, nsem.at[0])
    keep.start()

    def finish(p, carry):
        for k in range(chans):
            if k != me:
                q_send(p, k).wait_send()
                g_send(p, k).wait_send()
            kv_keep(p, k).wait()
            r_send(0, p, k).wait()
            r_send(1, p, k).wait()
        for cp in edges(p):
            cp.wait()

        @pl.when(c == chans - 1)
        def _():
            e_wrap(p).wait()

        @pl.when(c < chans - 1)
        def _():
            e_send(p, me).wait()

        hy_keep(p).wait()
        return carry

    lax.fori_loop(0, pieces, finish, 0)
    keep.wait()


def last_kernel(fq, g, ge, kv, kvx, tapsx, fm, hy, out, hy_out, gs):
    rows = out.shape[1]
    f32 = jnp.float32
    hy_out[...] = hy[...]
    out[0] = fq[...]
    for t in range(out.shape[2] // LANES):
        at = pl.ds(t * LANES, LANES)
        top = g[:, at].astype(f32)
        end = ge[:, at].astype(f32)
        for m in (1, 2):
            z = 2 * (t % 2) + m - 1
            gs[z, pl.ds(0, rows), :] = top * kv[2 - m, :, at]
            gs[z, pl.ds(rows, EDGE), :] = end * kvx[2 - m, :, at]
            tap = lambda j: tapsx[8 * m + j : 8 * m + j + 1, at]
            total = tap(0) * gs[z, pl.ds(0, rows), :]
            for j in range(1, SHORT):
                total = total + tap(j) * (fm[j - 1, pl.ds(j, rows), :] * gs[z, pl.ds(j, rows), :])
            out[m, :, at] = total.astype(jnp.bfloat16)


def solution(mesh):
    chans, seqs = mesh.shape["chan"], mesh.shape["seq"]

    def body(features, cotangent, short_filter, medium_filter, doc_start):
        own, width = cotangent.shape
        rows, _, full = features.shape
        groups = medium_filter.shape[0]
        span = full // (groups * chans)
        more = rows + EDGE
        bf, f32 = jnp.bfloat16, jnp.float32
        shape = jax.ShapeDtypeStruct
        dma = lambda *dims: pltpu.SemaphoreType.DMA(dims)
        x = jnp.transpose(features, (1, 0, 2))
        ctaps = jnp.transpose(short_filter, (0, 2, 1))
        limit = 60 << 20
        tiles = width // LANES
        pieces = min(PIECES, tiles)
        wide = min(WIDE, width)
        blocks = own // MEDIUM
        per = LANES // span
        vm = pltpu.VMEM

        hy, fq, back, bedge, kv, kvx, tapsx, fm = pl.pallas_call(
            functools.partial(core_kernel, chans, seqs, span, pieces),
            out_shape=(
                shape((own, width), bf), shape((rows, full), bf), shape((rows, full), bf), shape((EDGE, full), bf),
                shape((2, rows, full), f32), shape((2, EDGE, full), f32), shape((chans, 24, width), f32), shape((SHORT - 1, more, LANES), f32)),
            in_specs=[ANY, ANY, VMEM, VMEM, pl.BlockSpec(memory_space=pltpu.SMEM)],
            out_specs=(ANY,) * 6 + (VMEM, VMEM),
            scratch_shapes=[
                vm((2, rows, full), bf), vm((2, EDGE, full), bf), vm((2, EDGE, full), bf),
                vm((chans, 3, 8, groups), f32), vm((own, width), bf), vm((TAIL + own, width), bf),
                vm((rows, full), bf), vm((MEDIUM + own, width), bf), vm((own + MEDIUM, width), bf),
                vm((2, rows, full), f32), vm((2, EDGE, full), f32), vm((4, rows + EDGE, LANES), f32),
                vm((2, 2 * EDGE, LANES), f32), vm((TAIL + own, LANES), f32),
                vm((own, width), f32), vm((SHORT - 1, own + EDGE, LANES), f32),
                vm((blocks, MEDIUM, 2 * MEDIUM), bf), vm((blocks, MEDIUM, 2 * MEDIUM), bf),
                vm((blocks, per * MEDIUM, 2 * MEDIUM), bf), vm((groups, MEDIUM), f32), vm((groups, MEDIUM), f32),
                vm((2, own, width), bf), vm((own + EDGE, width), f32), vm((own, width), bf),
                dma(2), dma(2), dma(chans), dma(chans), dma(2),
                dma(pieces, chans), dma(pieces, chans), dma(pieces, chans), dma(pieces, chans), dma(1),
                dma(4, pieces), dma(4, pieces), dma(2, pieces, chans), dma(2, pieces, chans), dma(2, pieces),
                dma(pieces, chans), dma(pieces, chans), dma(pieces), dma(pieces, chans), dma(pieces),
            ],
            compiler_params=pltpu.CompilerParams(
                collective_id=0, has_side_effects=True, vmem_limit_bytes=limit),
            name="core",
        )(x, cotangent, ctaps, medium_filter, doc_start)

        per_owner = width // wide
        slab = pl.BlockSpec((own * wide // full, width), lambda i: (i, 0))
        flat = lambda n: pl.BlockSpec((n, wide), lambda i: (0, i))
        cube = lambda m, n: pl.BlockSpec((m, n, wide), lambda i: (0, 0, i))
        grad, hy = pl.pallas_call(
            last_kernel,
            grid=(full // wide,),
            out_shape=(shape((3, rows, full), bf), shape((own, width), bf)),
            in_specs=[
                flat(rows), flat(rows), flat(EDGE), cube(2, rows), cube(2, EDGE),
                pl.BlockSpec((None, 24, wide), lambda i: (i // per_owner, 0, i % per_owner)),
                pl.BlockSpec(fm.shape, lambda i: (0, 0, 0)), slab,
            ],
            out_specs=(cube(3, rows), slab),
            scratch_shapes=[vm((4, more, LANES), f32)],
            compiler_params=pltpu.CompilerParams(vmem_limit_bytes=limit),
            name="last_rows",
        )(fq, back, bedge, kv, kvx, tapsx, fm, hy)
        return hy, jnp.transpose(grad, (1, 0, 2))

    in_specs = (
        P(("seq", "chan"), None, None),
        P("seq", "chan"),
        P(None, "chan", None),
        P("chan", None),
        P(),
    )
    out_specs = (P("seq", "chan"), P(("seq", "chan"), None, None))
    return jax.shard_map(body, mesh=mesh, in_specs=in_specs, out_specs=out_specs, check_vma=False)
```

```python
import functools

import jax
import jax.numpy as jnp
from jax import lax
from jax.experimental import pallas as pl
from jax.experimental.pallas import tpu as pltpu
from jax.sharding import PartitionSpec as P

SHORT = 7
MEDIUM = 128
EDGE = 8
TAIL = 16
LANES = 128
PIECES = 8
AHEAD = 4
SKEW = 3
HOLD = 4
FAR = 1 << 20
MESH = pl.DeviceIdType.MESH
ANY = pl.BlockSpec(memory_space=pl.ANY)
VMEM = pl.BlockSpec(memory_space=pltpu.VMEM)


def remote(src, dst, ssem, rsem, dev):
    return pltpu.make_async_remote_copy(src, dst, ssem, rsem, device_id=dev, device_id_type=MESH)


def al(i, n):
    return pl.multiple_of(i, n)


def split3(t):
    bf, f32 = jnp.bfloat16, jnp.float32
    high = t.astype(bf)
    rest = t - high.astype(f32)
    mid = rest.astype(bf)
    low = (rest - mid.astype(f32)).astype(bf)
    return high, mid, low


def core_kernel(chans, seqs, span, pieces, x, cot, ctaps, filt, doc, hy, out,
                back, bedge, tapsx, fm, outv, xk, xprev, xnext, tall, cotv, q, gbuf, gat, gl, kvv, kvxv, xs, gs, xe, xq, sh, fmq, mf, mb, lf, filtf, filtr, sent, gq,
                hyv,
                esem, fsem, tsem, trsem, lsem, qss, qrs, gss, grs, nsem, hss, hrs, rss, rrs, rls, bss, brs, bls, ksem,
                ysem):
    c, s = lax.axis_index("chan"), lax.axis_index("seq")
    f32, bf = jnp.float32, jnp.bfloat16
    rows = x.shape[1]
    full = x.shape[2]
    more = rows + EDGE
    own, width = cot.shape
    groups = filt.shape[0]
    pw = width // pieces
    tp = pw // LANES
    half = chans // 2
    me = chans - 2
    start = s * own

    bar = pltpu.get_barrier_semaphore()
    for k in range(1, chans):
        pl.semaphore_signal(bar, inc=1, device_id={"chan": lax.rem(c + k, chans)}, device_id_type=MESH)
    for step in (1, seqs - 1):
        for k in range(chans):
            dev = {"seq": lax.rem(s + step, seqs), "chan": lax.rem(c + k, chans)}
            pl.semaphore_signal(bar, inc=1, device_id=dev, device_id_type=MESH)
    up, down = {"seq": lax.rem(s + 1, seqs)}, {"seq": lax.rem(s + seqs - 1, seqs)}
    after = {"seq": lax.rem(s + (c + 1) // chans, seqs), "chan": lax.rem(c + 1, chans)}
    ahead = {"seq": lax.rem(s + seqs - 1 + (c + chans - 1) // chans, seqs), "chan": lax.rem(c + chans - 1, chans)}

    def owner(k):
        return lax.rem(c // 2 + 1 + k // 2, half) * 2 + lax.rem(lax.rem(c, 2) + lax.rem(k, 2), 2)

    mine = pl.ds(al(TAIL + c * rows, 16), rows)
    gmine = pl.ds(al(MEDIUM + c * rows, 16), rows)

    def cols(d, p):
        return pl.ds(al(d * width + p * pw, LANES), pw)

    def part(p):
        return pl.ds(al(p * pw, LANES), pw)

    def q_send(p, k):
        d = owner(k)
        if k == me:
            return pltpu.make_async_copy(x.at[0, :, cols(d, p)], q.at[mine, part(p)], qrs.at[p, k])
        return remote(x.at[0, :, cols(d, p)], q.at[mine, part(p)], qss.at[p, k], qrs.at[p, k], {"chan": d})

    def g_send(p, k):
        d = owner(k)
        if k == me:
            return pltpu.make_async_copy(gbuf.at[:, cols(d, p)], gat.at[gmine, part(p)], grs.at[p, k])
        return remote(gbuf.at[:, cols(d, p)], gat.at[gmine, part(p)], gss.at[p, k], grs.at[p, k], {"chan": d})

    def out_keep(p, k):
        at = cols(owner(k), p)
        return pltpu.make_async_copy(outv.at[:, :, at], out.at[pl.ds(1, 2), :, at], ksem.at[p, k])

    def q_up(p):
        return remote(q.at[pl.ds(own, TAIL), part(p)], q.at[pl.ds(0, TAIL), part(p)], hss.at[0, p], hrs.at[0, p], up)

    def g_up(p):
        return remote(gat.at[pl.ds(own, MEDIUM), part(p)], gat.at[pl.ds(0, MEDIUM), part(p)], hss.at[1, p],
                      hrs.at[1, p], up)

    def l_down(p):
        return remote(gl.at[pl.ds(0, MEDIUM), part(p)], gl.at[pl.ds(own, MEDIUM), part(p)], hss.at[2, p],
                      hrs.at[2, p], down)

    def gq_down(p):
        return remote(gq.at[pl.ds(0, EDGE), part(p)], gq.at[pl.ds(own, EDGE), part(p)], hss.at[3, p], hrs.at[3, p],
                      down)

    def r_send(m, p, k):
        d = owner(k)
        src = sent.at[m, pl.ds(al(d * rows, 16), rows), part(p)]
        dst = back.at[:, cols(c, p)] if m else out.at[0, :, cols(c, p)]
        if k == me:
            return pltpu.make_async_copy(src, dst, rls.at[m, p])
        return remote(src, dst, rss.at[m, p, k], rrs.at[m, p, k], {"chan": d})

    def e_send(p, k):
        d = owner(k)
        src = sent.at[1, pl.ds(al(lax.rem(d + 1, chans) * rows, 16), EDGE), part(p)]
        dst = bedge.at[:, cols(c, p)]
        if k == me:
            return pltpu.make_async_copy(src, dst, bls.at[p])
        dev = {"seq": lax.rem(s + seqs - (d + 1) // chans, seqs), "chan": d}
        return remote(src, dst, bss.at[p, k], brs.at[p, k], dev)

    def e_wrap(p):
        dev = {"seq": lax.rem(s + seqs - 1, seqs), "chan": c}
        return remote(sent.at[1, pl.ds(0, EDGE), part(p)], bedge.at[:, cols(c, p)], bss.at[p, me], brs.at[p, me], dev)

    loads = [
        pltpu.make_async_copy(x.at[pl.ds(1, 2)], xk, lsem.at[0]),
        pltpu.make_async_copy(cot, cotv, lsem.at[1]),
    ]
    for cp in loads:
        cp.start()

    tall[c] = jnp.zeros(tall.shape[1:], f32)
    tall[c, :, pl.ds(0, SHORT), :] = ctaps[...]

    low = jnp.maximum(s - 1, 0)
    high = jnp.minimum(s + 1, seqs - 1)
    b0 = (s - 1) * own + doc[low]
    b1 = s * own + doc[s]
    b2 = (s + 1) * own + doc[high]
    tokens = seqs * own

    def ids(pos):
        one = lambda b: jnp.where(pos >= b, 1, 0)
        seg = one(b0) + one(b1) + one(b2)
        return jnp.where(pos < 0, -1, jnp.where(pos >= tokens, FAR, seg))

    pl.semaphore_wait(bar, chans - 1 + 2 * chans)
    taps = []
    early = [
        remote(x.at[pl.ds(1, 2), pl.ds(rows - EDGE, EDGE)], xprev, esem.at[0], fsem.at[0], after),
    ]
    later = remote(x.at[pl.ds(1, 2), pl.ds(0, EDGE)], xnext, esem.at[1], fsem.at[1], ahead)
    for k in range(chans):
        if k != me:
            taps.append(remote(tall.at[c], tall.at[c], tsem.at[k], trsem.at[k], {"chan": owner(k)}))
    for cp in early + taps:
        cp.start()

    pos = start + c * rows + lax.broadcasted_iota(jnp.int32, (more, LANES), 0)
    here = ids(pos)
    for j in range(1, SHORT):
        fm[j - 1] = jnp.where(here == ids(pos - j), 1.0, 0.0)
    for p in range(min(AHEAD, pieces)):
        for k in range(chans):
            q_send(p, k).start()
    pos = start + lax.broadcasted_iota(jnp.int32, (own + EDGE, LANES), 0)
    here = ids(pos)
    for j in range(1, SHORT):
        fmq[j - 1] = jnp.where(here == ids(pos - j), 1.0, 0.0)
    r = lax.broadcasted_iota(jnp.int32, (MEDIUM, 2 * MEDIUM), 0)
    k2 = lax.broadcasted_iota(jnp.int32, (MEDIUM, 2 * MEDIUM), 1)
    for b in range(own // MEDIUM):
        base = start + b * MEDIUM
        here = ids(base + r)
        lag = r + MEDIUM - k2
        ok = (lag >= 0) & (lag < MEDIUM) & (here == ids(base - MEDIUM + k2))
        mf[b] = jnp.where(ok, 1.0, 0.0).astype(bf)
        lag = k2 - r
        ok = (lag >= 0) & (lag < MEDIUM) & (here == ids(base + k2))
        mb[b] = jnp.where(ok, 1.0, 0.0).astype(bf)
    rounded = filt[...].astype(bf)
    filtf[...] = rounded.astype(f32)
    ri = lax.broadcasted_iota(jnp.int32, (MEDIUM, MEDIUM), 0)
    ci = lax.broadcasted_iota(jnp.int32, (MEDIUM, MEDIUM), 1)
    turn = jnp.where(lax.rem(ri + ci, MEDIUM) == 0, 1.0, 0.0).astype(bf)
    filtr[...] = jnp.dot(rounded, turn, preferred_element_type=f32)

    for cp in taps:
        cp.wait()

    def widen(n, carry):
        at = n * pw
        row = lax.broadcasted_iota(jnp.int32, (groups, pw), 0)
        col = lax.broadcasted_iota(jnp.int32, (groups, pw), 1)
        hot = jnp.where(row == (at + col) // span, 1.0, 0.0).astype(bf)
        for d in range(chans):
            full_taps = tall[d].reshape(24, groups)
            high, mid, low3 = (jnp.dot(v, hot, preferred_element_type=f32) for v in split3(full_taps))
            tapsx[d, :, pl.ds(al(at, LANES), pw)] = high + (mid + low3)
        return carry

    lax.fori_loop(0, pieces, widen, 0)
    for cp in loads + early:
        cp.wait()

    def chunk(n, carry):
        p, k = n // chans, lax.rem(n, chans)
        d = owner(k)
        for t in range(tp):
            lane = pl.ds(al(p * pw + t * LANES, LANES), LANES)
            at = pl.ds(al(d * width + p * pw + t * LANES, LANES), LANES)
            outs = []
            for m in range(2):
                z = 2 * (t % 2) + m
                xs[z, pl.ds(0, EDGE), :] = xprev[m, :, at].astype(f32)
                xs[z, pl.ds(EDGE, rows), :] = xk[m, :, at].astype(f32)
                tap = lambda j: tapsx[d, 8 * (m + 1) + j : 8 * (m + 1) + j + 1, lane]
                total = tap(0) * xs[z, pl.ds(EDGE, rows), :]
                for j in range(1, SHORT):
                    total = total + tap(j) * (fm[j - 1, pl.ds(0, rows), :] * xs[z, pl.ds(EDGE - j, rows), :])
                kvv[m, :, at] = total
                outs.append(total)
            gbuf[:, at] = (outs[0] * outs[1]).astype(bf)
        return carry

    def rowside(p, carry):
        lax.fori_loop(p * chans, (p + 1) * chans, chunk, 0)

        @pl.when(p < AHEAD)
        def _():
            for k in range(chans):
                g_send(p, k).start()

        return carry

    lax.fori_loop(0, pieces, rowside, 0)
    later.start()

    def beyond(n, carry):
        d, at0 = n // (pieces * tp), lax.rem(n, pieces * tp)
        lane = pl.ds(al(at0 * LANES, LANES), LANES)
        at = pl.ds(al(n * LANES, LANES), LANES)
        for m in range(2):
            xe[m, pl.ds(0, EDGE), :] = xk[m, pl.ds(rows - EDGE, EDGE), at].astype(f32)
            xe[m, pl.ds(EDGE, EDGE), :] = xnext[m, :, at].astype(f32)
            tap = lambda j: tapsx[d, 8 * (m + 1) + j : 8 * (m + 1) + j + 1, lane]
            total = tap(0) * xe[m, pl.ds(EDGE, EDGE), :]
            for j in range(1, SHORT):
                total = total + tap(j) * (fm[j - 1, pl.ds(rows, EDGE), :] * xe[m, pl.ds(EDGE - j, EDGE), :])
            kvxv[m, :, at] = total
        return carry

    lane_group = lax.broadcasted_iota(jnp.int32, (MEDIUM, LANES), 1) // span
    per = LANES // span
    blocks = own // MEDIUM

    def query(t, carry):
        at = pl.ds(al(t * LANES, LANES), LANES)
        xq[...] = q[:, at].astype(f32)
        step = 64
        for lo in range(0, own, step):
            tap = lambda j: tapsx[c, j : j + 1, at]
            total = tap(0) * xq[pl.ds(TAIL + lo, step), :]
            for j in range(1, SHORT):
                total = total + tap(j) * (fmq[j - 1, pl.ds(lo, step), :] * xq[pl.ds(TAIL + lo - j, step), :])
            sh[pl.ds(lo, step), at] = total
            gl[pl.ds(lo, step), at] = (cotv[pl.ds(lo, step), at].astype(f32) * total).astype(bf)
        return carry

    def band(filters, masks):
        for g in range(per):
            row = jnp.broadcast_to(filters[g : g + 1, :], (MEDIUM, MEDIUM))
            circ = pltpu.roll(row, 0, 1, stride=1, stride_axis=0).astype(bf)
            two = jnp.concatenate([circ, circ], axis=1)
            for b in range(blocks):
                lf[b, pl.ds(g * MEDIUM, MEDIUM), :] = two * masks[b]

    def product(b, source, at):
        rhs = source[pl.ds(MEDIUM * b, 2 * MEDIUM), at]
        res = jnp.dot(lf[b], rhs, preferred_element_type=f32)
        total = res[:MEDIUM]
        for g in range(1, per):
            total = jnp.where(lane_group == g, res[g * MEDIUM : (g + 1) * MEDIUM], total)
        return total

    def forward(t, carry):
        at = pl.ds(al(t * LANES, LANES), LANES)
        band(filtr[pl.ds(al(t * per, per), per), :], mf)
        for b in range(blocks):
            long = product(b, gat, at)
            lo = pl.ds(MEDIUM * b, MEDIUM)
            hyv[lo, at] = (sh[lo, at] * long).astype(bf)
            gq[lo, at] = cotv[lo, at].astype(f32) * long
        return carry

    def backward(t, carry):
        at = pl.ds(al(t * LANES, LANES), LANES)
        band(filtf[pl.ds(al(t * per, per), per), :], mb)
        for b in range(blocks):
            sent[1, pl.ds(MEDIUM * b, MEDIUM), at] = product(b, gl, at).astype(bf)
        return carry

    def query_back(t, carry):
        at = pl.ds(al(t * LANES, LANES), LANES)
        xq[pl.ds(0, own + EDGE), :] = gq[:, at]
        step = 64
        for lo in range(0, own, step):
            tap = lambda j: tapsx[c, j : j + 1, at]
            total = tap(0) * xq[pl.ds(lo, step), :]
            for j in range(1, SHORT):
                total = total + tap(j) * (fmq[j - 1, pl.ds(lo + j, step), :] * xq[pl.ds(lo + j, step), :])
            sent[0, pl.ds(lo, step), at] = total.astype(bf)
        return carry

    def edges(p):
        return [e_send(p, k) for k in range(chans) if k != me]

    def hy_keep(p):
        return pltpu.make_async_copy(hyv.at[:, part(p)], hy.at[:, part(p)], ysem.at[p])

    def give(p, carry):
        for k in range(chans):
            r_send(1, p, k).start()
        for cp in edges(p):
            cp.start()

        @pl.when(c == chans - 1)
        def _():
            e_wrap(p).start()

        @pl.when(c < chans - 1)
        def _():
            e_send(p, me).start()

        for k in range(chans):
            r_send(0, p, k).start()
        return carry

    hold = max(SKEW, pieces - HOLD)

    def stage(p, carry):
        @pl.when(p < pieces)
        def _():
            for k in range(chans):
                q_send(p, k).wait() if k == me else q_send(p, k).wait_recv()
            q_up(p).start()
            for k in range(chans):
                g_send(p, k).wait() if k == me else g_send(p, k).wait_recv()
            g_up(p).start()

        @pl.when(p + AHEAD < pieces)
        def _():
            for k in range(chans):
                q_send(p + AHEAD, k).start()
            for k in range(chans):
                g_send(p + AHEAD, k).start()

        @pl.when(p == hold)
        def _():
            lax.fori_loop(0, hold - SKEW, give, 0)

        @pl.when((p > 0) & (p <= pieces))
        def _():
            q_up(p - 1).wait()
            lax.fori_loop((p - 1) * tp, p * tp, query, 0)
            l_down(p - 1).start()

        @pl.when((p >= SKEW - 1) & (p < pieces + SKEW - 1))
        def _():
            f = p - SKEW + 1
            g_up(f).wait()
            lax.fori_loop(f * tp, (f + 1) * tp, forward, 0)
            gq_down(f).start()
            hy_keep(f).start()

        @pl.when(p >= SKEW)
        def _():
            f = p - SKEW
            l_down(f).wait()
            lax.fori_loop(f * tp, (f + 1) * tp, backward, 0)
            gq_down(f).wait()
            lax.fori_loop(f * tp, (f + 1) * tp, query_back, 0)

            @pl.when(p >= hold)
            def _():
                give(f, 0)

        return carry

    lax.fori_loop(0, pieces + SKEW, stage, 0)
    later.wait()
    lax.fori_loop(0, chans * pieces * tp, beyond, 0)
    def turned(n, carry):
        p, k = n // chans, lax.rem(n, chans)
        d = owner(k)
        for t in range(tp):
            lane = pl.ds(al(p * pw + t * LANES, LANES), LANES)
            at = pl.ds(al(d * width + p * pw + t * LANES, LANES), LANES)
            top = back[:, at].astype(f32)
            end = bedge[:, at].astype(f32)
            for m in range(2):
                z = 2 * (t % 2) + m
                gs[z, pl.ds(0, rows), :] = top * kvv[1 - m, :, at]
                gs[z, pl.ds(rows, EDGE), :] = end * kvxv[1 - m, :, at]
                tap = lambda j: tapsx[d, 8 * (m + 1) + j : 8 * (m + 1) + j + 1, lane]
                total = tap(0) * gs[z, pl.ds(0, rows), :]
                for j in range(1, SHORT):
                    total = total + tap(j) * (fm[j - 1, pl.ds(j, rows), :] * gs[z, pl.ds(j, rows), :])
                outv[m, :, at] = total.astype(bf)
        out_keep(p, k).start()
        return carry

    def come(p, carry):
        for k in range(chans):
            if k == me:
                r_send(1, p, k).wait()
            else:
                r_send(1, p, k).wait_recv()
                e_send(p, k).wait_recv()

        @pl.when(c == chans - 1)
        def _():
            e_wrap(p).wait_recv()

        @pl.when(c < chans - 1)
        def _():
            e_send(p, me).wait()

        lax.fori_loop(p * chans, (p + 1) * chans, turned, 0)
        return carry

    lax.fori_loop(0, pieces, come, 0)

    def finish(p, carry):
        for k in range(chans):
            if k != me:
                q_send(p, k).wait_send()
                g_send(p, k).wait_send()
                r_send(1, p, k).wait_send()
                e_send(p, k).wait_send()
            out_keep(p, k).wait()
            r_send(0, p, k).wait()

        @pl.when(c == chans - 1)
        def _():
            e_wrap(p).wait_send()

        hy_keep(p).wait()
        return carry

    lax.fori_loop(0, pieces, finish, 0)


def copy_kernel(a, b, a_out, b_out, av, bv, isem, osem):
    parts = [(a.at[i], av.at[i], a_out.at[i]) for i in range(3)]
    half = b.shape[0] // 2
    parts += [tuple(r.at[pl.ds(i * half, half)] for r in (b, bv, b_out)) for i in range(2)]
    ins, outs = [], []
    for i, (src, mid, dst) in enumerate(parts):
        ins.append(pltpu.make_async_copy(src, mid, isem.at[i]))
        outs.append(pltpu.make_async_copy(mid, dst, osem.at[i]))
        ins[i].start()
    for come, go in zip(ins, outs):
        come.wait()
        go.start()
    for go in outs:
        go.wait()


def solution(mesh):
    chans, seqs = mesh.shape["chan"], mesh.shape["seq"]

    def body(features, cotangent, short_filter, medium_filter, doc_start):
        own, width = cotangent.shape
        rows, _, full = features.shape
        groups = medium_filter.shape[0]
        span = full // (groups * chans)
        more = rows + EDGE
        bf, f32 = jnp.bfloat16, jnp.float32
        shape = jax.ShapeDtypeStruct
        dma = lambda *dims: pltpu.SemaphoreType.DMA(dims)
        x = jnp.transpose(features, (1, 0, 2))
        ctaps = jnp.transpose(short_filter, (0, 2, 1))
        limit = 60 << 20
        tiles = width // LANES
        pieces = min(PIECES, tiles)
        blocks = own // MEDIUM
        per = LANES // span
        vm = pltpu.VMEM

        hy, grad = pl.pallas_call(
            functools.partial(core_kernel, chans, seqs, span, pieces),
            out_shape=(shape((own, width), bf), shape((3, rows, full), bf)),
            in_specs=[ANY, ANY, VMEM, VMEM, pl.BlockSpec(memory_space=pltpu.SMEM)],
            out_specs=(ANY, ANY),
            scratch_shapes=[
                vm((rows, full), bf), vm((EDGE, full), bf), vm((chans, 24, width), f32), vm((SHORT - 1, more, LANES), f32),
                vm((2, rows, full), bf), vm((2, rows, full), bf), vm((2, EDGE, full), bf), vm((2, EDGE, full), bf),
                vm((chans, 3, 8, groups), f32), vm((own, width), bf), vm((TAIL + own, width), bf),
                vm((rows, full), bf), vm((MEDIUM + own, width), bf), vm((own + MEDIUM, width), bf),
                vm((2, rows, full), f32), vm((2, EDGE, full), f32), vm((4, rows + EDGE, LANES), f32), vm((4, more, LANES), f32),
                vm((2, 2 * EDGE, LANES), f32), vm((TAIL + own, LANES), f32),
                vm((own, width), f32), vm((SHORT - 1, own + EDGE, LANES), f32),
                vm((blocks, MEDIUM, 2 * MEDIUM), bf), vm((blocks, MEDIUM, 2 * MEDIUM), bf),
                vm((blocks, per * MEDIUM, 2 * MEDIUM), bf), vm((groups, MEDIUM), f32), vm((groups, MEDIUM), f32),
                vm((2, own, width), bf), vm((own + EDGE, width), f32), vm((own, width), bf),
                dma(2), dma(2), dma(chans), dma(chans), dma(2),
                dma(pieces, chans), dma(pieces, chans), dma(pieces, chans), dma(pieces, chans), dma(1),
                dma(4, pieces), dma(4, pieces), dma(2, pieces, chans), dma(2, pieces, chans), dma(2, pieces),
                dma(pieces, chans), dma(pieces, chans), dma(pieces), dma(pieces, chans), dma(pieces),
            ],
            compiler_params=pltpu.CompilerParams(
                collective_id=0, has_side_effects=True, vmem_limit_bytes=limit),
            name="core",
        )(x, cotangent, ctaps, medium_filter, doc_start)

        grad, hy = pl.pallas_call(
            copy_kernel,
            out_shape=(shape((3, rows, full), bf), shape((own, width), bf)),
            in_specs=[ANY, ANY],
            out_specs=(ANY, ANY),
            scratch_shapes=[vm((3, rows, full), bf), vm((own, width), bf), dma(5), dma(5)],
            compiler_params=pltpu.CompilerParams(vmem_limit_bytes=limit),
            name="hand_out",
        )(grad, hy)
        return hy, jnp.transpose(grad, (1, 0, 2))

    in_specs = (
        P(("seq", "chan"), None, None),
        P("seq", "chan"),
        P(None, "chan", None),
        P("chan", None),
        P(),
    )
    out_specs = (P("seq", "chan"), P(("seq", "chan"), None, None))
    return jax.shard_map(body, mesh=mesh, in_specs=in_specs, out_specs=out_specs, check_vma=False)
```

```python
import functools

import jax
import jax.numpy as jnp
from jax import lax
from jax.experimental import pallas as pl
from jax.experimental.pallas import tpu as pltpu
from jax.sharding import PartitionSpec as P

SHORT = 7
MEDIUM = 128
EDGE = 8
TAIL = 16
LANES = 128
PIECES = 8
AHEAD = 4
LEAD = 1
QUEUE = 4
FAR = 1 << 20
MESH = pl.DeviceIdType.MESH
ANY = pl.BlockSpec(memory_space=pl.ANY)
VMEM = pl.BlockSpec(memory_space=pltpu.VMEM)


def remote(src, dst, ssem, rsem, dev):
    return pltpu.make_async_remote_copy(src, dst, ssem, rsem, device_id=dev, device_id_type=MESH)


def al(i, n):
    return pl.multiple_of(i, n)


def split3(t):
    bf, f32 = jnp.bfloat16, jnp.float32
    high = t.astype(bf)
    rest = t - high.astype(f32)
    mid = rest.astype(bf)
    low = (rest - mid.astype(f32)).astype(bf)
    return high, mid, low


def core_kernel(chans, seqs, span, pieces, x, cot, ctaps_hbm, filt_hbm, doc_hbm, hy, out, ctaps, filt, doc,
                back, bedge, tapsx, fm, xk, xprev, xnext, tall, cotv, q, gbuf, gat, gl, kvv, kvxv, xs, gs, xe, xq, sh, fmq, mf, mb, lf, filtf, filtr, sent, gq,
                esem, fsem, tsem, trsem, lsem, qss, qrs, gss, grs, nsem, hss, hrs, rss, rrs, rls, bss, brs, bls):
    c, s = lax.axis_index("chan"), lax.axis_index("seq")
    f32, bf = jnp.float32, jnp.bfloat16
    rows = x.shape[1]
    full = x.shape[2]
    more = rows + EDGE
    own, width = cot.shape
    groups = filt.shape[0]
    pw = width // pieces
    tp = pw // LANES
    half = chans // 2
    me = chans - 2
    start = s * own

    bar = pltpu.get_barrier_semaphore()
    for k in range(1, chans):
        pl.semaphore_signal(bar, inc=1, device_id={"chan": lax.rem(c + k, chans)}, device_id_type=MESH)
    for step in (1, seqs - 1):
        for k in range(chans):
            dev = {"seq": lax.rem(s + step, seqs), "chan": lax.rem(c + k, chans)}
            pl.semaphore_signal(bar, inc=1, device_id=dev, device_id_type=MESH)
    up, down = {"seq": lax.rem(s + 1, seqs)}, {"seq": lax.rem(s + seqs - 1, seqs)}
    after = {"seq": lax.rem(s + (c + 1) // chans, seqs), "chan": lax.rem(c + 1, chans)}
    ahead = {"seq": lax.rem(s + seqs - 1 + (c + chans - 1) // chans, seqs), "chan": lax.rem(c + chans - 1, chans)}

    def owner(k):
        return lax.rem(c // 2 + 1 + k // 2, half) * 2 + lax.rem(lax.rem(c, 2) + lax.rem(k, 2), 2)

    mine = pl.ds(al(TAIL + c * rows, 16), rows)
    gmine = pl.ds(al(MEDIUM + c * rows, 16), rows)

    def cols(d, p):
        return pl.ds(al(d * width + p * pw, LANES), pw)

    def part(p):
        return pl.ds(al(p * pw, LANES), pw)

    def q_send(p, k):
        d = owner(k)
        if k == me:
            return pltpu.make_async_copy(x.at[0, :, cols(d, p)], q.at[mine, part(p)], qrs.at[p, k])
        return remote(x.at[0, :, cols(d, p)], q.at[mine, part(p)], qss.at[p, k], qrs.at[p, k], {"chan": d})

    def g_send(p, k):
        d = owner(k)
        if k == me:
            return pltpu.make_async_copy(gbuf.at[:, cols(d, p)], gat.at[gmine, part(p)], grs.at[p, k])
        return remote(gbuf.at[:, cols(d, p)], gat.at[gmine, part(p)], gss.at[p, k], grs.at[p, k], {"chan": d})

    def q_up(p):
        return remote(q.at[pl.ds(own, TAIL), part(p)], q.at[pl.ds(0, TAIL), part(p)], hss.at[0, p], hrs.at[0, p], up)

    def g_up(p):
        return remote(gat.at[pl.ds(own, MEDIUM), part(p)], gat.at[pl.ds(0, MEDIUM), part(p)], hss.at[1, p],
                      hrs.at[1, p], up)

    def l_down(p):
        return remote(gl.at[pl.ds(0, MEDIUM), part(p)], gl.at[pl.ds(own, MEDIUM), part(p)], hss.at[2, p],
                      hrs.at[2, p], down)

    def gq_down(p):
        return remote(gq.at[pl.ds(0, EDGE), part(p)], gq.at[pl.ds(own, EDGE), part(p)], hss.at[3, p], hrs.at[3, p],
                      down)

    def r_send(m, p, k):
        d = owner(k)
        src = sent.at[m, pl.ds(al(d * rows, 16), rows), part(p)]
        dst = back.at[:, cols(c, p)] if m else out.at[0, :, cols(c, p)]
        if k == me:
            return pltpu.make_async_copy(src, dst, rls.at[m, p])
        return remote(src, dst, rss.at[m, p, k], rrs.at[m, p, k], {"chan": d})

    def e_send(p, k):
        d = owner(k)
        src = sent.at[1, pl.ds(al(lax.rem(d + 1, chans) * rows, 16), EDGE), part(p)]
        dst = bedge.at[:, cols(c, p)]
        if k == me:
            return pltpu.make_async_copy(src, dst, bls.at[p])
        dev = {"seq": lax.rem(s + seqs - (d + 1) // chans, seqs), "chan": d}
        return remote(src, dst, bss.at[p, k], brs.at[p, k], dev)

    def e_wrap(p):
        dev = {"seq": lax.rem(s + seqs - 1, seqs), "chan": c}
        return remote(sent.at[1, pl.ds(0, EDGE), part(p)], bedge.at[:, cols(c, p)], bss.at[p, me], brs.at[p, me], dev)

    loads = [
        pltpu.make_async_copy(x.at[pl.ds(1, 2)], xk, lsem.at[0]),
        pltpu.make_async_copy(cot, cotv, lsem.at[1]),
    ]
    small = [
        pltpu.make_async_copy(ctaps_hbm, ctaps, lsem.at[2]),
        pltpu.make_async_copy(filt_hbm, filt, lsem.at[3]),
        pltpu.make_async_copy(doc_hbm, doc, lsem.at[4]),
    ]
    for cp in small + loads:
        cp.start()

    tall[c] = jnp.zeros(tall.shape[1:], f32)

    pl.semaphore_wait(bar, chans - 1 + 2 * chans)
    taps = []
    early = [
        remote(x.at[pl.ds(1, 2), pl.ds(rows - EDGE, EDGE)], xprev, esem.at[0], fsem.at[0], after),
    ]
    later = remote(x.at[pl.ds(1, 2), pl.ds(0, EDGE)], xnext, esem.at[1], fsem.at[1], ahead)
    for k in range(chans):
        if k != me:
            taps.append(remote(tall.at[c], tall.at[c], tsem.at[k], trsem.at[k], {"chan": owner(k)}))
    for cp in early:
        cp.start()
    for cp in small:
        cp.wait()
    tall[c, :, pl.ds(0, SHORT), :] = ctaps[...]
    for cp in taps:
        cp.start()
    for p in range(min(QUEUE, pieces)):
        for k in range(chans):
            q_send(p, k).start()

    low = jnp.maximum(s - 1, 0)
    high = jnp.minimum(s + 1, seqs - 1)
    b0 = (s - 1) * own + doc[low]
    b1 = s * own + doc[s]
    b2 = (s + 1) * own + doc[high]
    tokens = seqs * own

    def ids(pos):
        one = lambda b: jnp.where(pos >= b, 1, 0)
        seg = one(b0) + one(b1) + one(b2)
        return jnp.where(pos < 0, -1, jnp.where(pos >= tokens, FAR, seg))

    pos = start + c * rows + lax.broadcasted_iota(jnp.int32, (more, LANES), 0)
    here = ids(pos)
    for j in range(1, SHORT):
        fm[j - 1] = jnp.where(here == ids(pos - j), 1.0, 0.0)
    pos = start + lax.broadcasted_iota(jnp.int32, (own + EDGE, LANES), 0)
    here = ids(pos)
    for j in range(1, SHORT):
        fmq[j - 1] = jnp.where(here == ids(pos - j), 1.0, 0.0)
    r = lax.broadcasted_iota(jnp.int32, (MEDIUM, 2 * MEDIUM), 0)
    k2 = lax.broadcasted_iota(jnp.int32, (MEDIUM, 2 * MEDIUM), 1)
    for b in range(own // MEDIUM):
        base = start + b * MEDIUM
        here = ids(base + r)
        lag = r + MEDIUM - k2
        ok = (lag >= 0) & (lag < MEDIUM) & (here == ids(base - MEDIUM + k2))
        mf[b] = jnp.where(ok, 1.0, 0.0).astype(bf)
        lag = k2 - r
        ok = (lag >= 0) & (lag < MEDIUM) & (here == ids(base + k2))
        mb[b] = jnp.where(ok, 1.0, 0.0).astype(bf)
    rounded = filt[...].astype(bf)
    filtf[...] = rounded.astype(f32)
    ri = lax.broadcasted_iota(jnp.int32, (MEDIUM, MEDIUM), 0)
    ci = lax.broadcasted_iota(jnp.int32, (MEDIUM, MEDIUM), 1)
    turn = jnp.where(lax.rem(ri + ci, MEDIUM) == 0, 1.0, 0.0).astype(bf)
    filtr[...] = jnp.dot(rounded, turn, preferred_element_type=f32)

    for cp in taps:
        cp.wait()

    def widen(n, carry):
        at = n * pw
        row = lax.broadcasted_iota(jnp.int32, (groups, pw), 0)
        col = lax.broadcasted_iota(jnp.int32, (groups, pw), 1)
        hot = jnp.where(row == (at + col) // span, 1.0, 0.0).astype(bf)
        for d in range(chans):
            full_taps = tall[d].reshape(24, groups)
            high, mid, low3 = (jnp.dot(v, hot, preferred_element_type=f32) for v in split3(full_taps))
            tapsx[d, :, pl.ds(al(at, LANES), pw)] = high + (mid + low3)
        return carry

    lax.fori_loop(0, pieces, widen, 0)
    for cp in loads + early:
        cp.wait()

    def chunk(n, carry):
        p, k = n // chans, lax.rem(n, chans)
        d = owner(k)
        for t in range(tp):
            lane = pl.ds(al(p * pw + t * LANES, LANES), LANES)
            at = pl.ds(al(d * width + p * pw + t * LANES, LANES), LANES)
            outs = []
            for m in range(2):
                z = 2 * (t % 2) + m
                xs[z, pl.ds(0, EDGE), :] = xprev[m, :, at].astype(f32)
                xs[z, pl.ds(EDGE, rows), :] = xk[m, :, at].astype(f32)
                tap = lambda j: tapsx[d, 8 * (m + 1) + j : 8 * (m + 1) + j + 1, lane]
                total = tap(0) * xs[z, pl.ds(EDGE, rows), :]
                for j in range(1, SHORT):
                    total = total + tap(j) * (fm[j - 1, pl.ds(0, rows), :] * xs[z, pl.ds(EDGE - j, rows), :])
                kvv[m, :, at] = total
                outs.append(total)
            gbuf[:, at] = (outs[0] * outs[1]).astype(bf)
        return carry

    def rowside(p, carry):
        lax.fori_loop(p * chans, (p + 1) * chans, chunk, 0)

        @pl.when(p < AHEAD)
        def _():
            for k in range(chans):
                g_send(p, k).start()

        return carry

    lax.fori_loop(0, pieces, rowside, 0)
    later.start()

    def beyond(n, carry):
        d, at0 = n // (pieces * tp), lax.rem(n, pieces * tp)
        lane = pl.ds(al(at0 * LANES, LANES), LANES)
        at = pl.ds(al(n * LANES, LANES), LANES)
        for m in range(2):
            xe[m, pl.ds(0, EDGE), :] = xk[m, pl.ds(rows - EDGE, EDGE), at].astype(f32)
            xe[m, pl.ds(EDGE, EDGE), :] = xnext[m, :, at].astype(f32)
            tap = lambda j: tapsx[d, 8 * (m + 1) + j : 8 * (m + 1) + j + 1, lane]
            total = tap(0) * xe[m, pl.ds(EDGE, EDGE), :]
            for j in range(1, SHORT):
                total = total + tap(j) * (fm[j - 1, pl.ds(rows, EDGE), :] * xe[m, pl.ds(EDGE - j, EDGE), :])
            kvxv[m, :, at] = total
        return carry

    lane_group = lax.broadcasted_iota(jnp.int32, (MEDIUM, LANES), 1) // span
    per = LANES // span
    blocks = own // MEDIUM

    def query(t, carry):
        at = pl.ds(al(t * LANES, LANES), LANES)
        xq[...] = q[:, at].astype(f32)
        step = 64
        for lo in range(0, own, step):
            tap = lambda j: tapsx[c, j : j + 1, at]
            total = tap(0) * xq[pl.ds(TAIL + lo, step), :]
            for j in range(1, SHORT):
                total = total + tap(j) * (fmq[j - 1, pl.ds(lo, step), :] * xq[pl.ds(TAIL + lo - j, step), :])
            sh[pl.ds(lo, step), at] = total
            gl[pl.ds(lo, step), at] = (cotv[pl.ds(lo, step), at].astype(f32) * total).astype(bf)
        return carry

    def band(filters, masks):
        for g in range(per):
            row = jnp.broadcast_to(filters[g : g + 1, :], (MEDIUM, MEDIUM))
            circ = pltpu.roll(row, 0, 1, stride=1, stride_axis=0).astype(bf)
            two = jnp.concatenate([circ, circ], axis=1)
            for b in range(blocks):
                lf[b, pl.ds(g * MEDIUM, MEDIUM), :] = two * masks[b]

    def product(b, source, at):
        rhs = source[pl.ds(MEDIUM * b, 2 * MEDIUM), at]
        res = jnp.dot(lf[b], rhs, preferred_element_type=f32)
        total = res[:MEDIUM]
        for g in range(1, per):
            total = jnp.where(lane_group == g, res[g * MEDIUM : (g + 1) * MEDIUM], total)
        return total

    def forward(t, carry):
        at = pl.ds(al(t * LANES, LANES), LANES)
        band(filtr[pl.ds(al(t * per, per), per), :], mf)
        for b in range(blocks):
            long = product(b, gat, at)
            lo = pl.ds(MEDIUM * b, MEDIUM)
            hy[lo, at] = (sh[lo, at] * long).astype(bf)
            gq[lo, at] = cotv[lo, at].astype(f32) * long
        return carry

    def backward(t, carry):
        at = pl.ds(al(t * LANES, LANES), LANES)
        band(filtf[pl.ds(al(t * per, per), per), :], mb)
        for b in range(blocks):
            sent[1, pl.ds(MEDIUM * b, MEDIUM), at] = product(b, gl, at).astype(bf)
        return carry

    def query_back(t, carry):
        at = pl.ds(al(t * LANES, LANES), LANES)
        xq[pl.ds(0, own + EDGE), :] = gq[:, at]
        step = 64
        for lo in range(0, own, step):
            tap = lambda j: tapsx[c, j : j + 1, at]
            total = tap(0) * xq[pl.ds(lo, step), :]
            for j in range(1, SHORT):
                total = total + tap(j) * (fmq[j - 1, pl.ds(lo + j, step), :] * xq[pl.ds(lo + j, step), :])
            sent[0, pl.ds(lo, step), at] = total.astype(bf)
        return carry

    def edges(p):
        return [e_send(p, k) for k in range(chans) if k != me]

    def give(p):
        for k in range(chans):
            r_send(1, p, k).start()
        for cp in edges(p):
            cp.start()

        @pl.when(c == chans - 1)
        def _():
            e_wrap(p).start()

        @pl.when(c < chans - 1)
        def _():
            e_send(p, me).start()

    def stage(i, carry):
        @pl.when(i < pieces)
        def _():
            for k in range(chans):
                q_send(i, k).wait() if k == me else q_send(i, k).wait_recv()
            q_up(i).start()

        @pl.when((i >= LEAD) & (i < pieces + LEAD))
        def _():
            p = i - LEAD
            for k in range(chans):
                g_send(p, k).wait() if k == me else g_send(p, k).wait_recv()
            g_up(p).start()

        @pl.when(i + QUEUE < pieces)
        def _():
            for k in range(chans):
                q_send(i + QUEUE, k).start()

        @pl.when((i >= LEAD) & (i - LEAD + AHEAD < pieces))
        def _():
            for k in range(chans):
                g_send(i - LEAD + AHEAD, k).start()

        @pl.when((i >= 1) & (i < pieces + 1))
        def _():
            p = i - 1
            q_up(p).wait()
            lax.fori_loop(p * tp, (p + 1) * tp, query, 0)
            l_down(p).start()

        @pl.when((i >= LEAD + 1) & (i < pieces + LEAD + 1))
        def _():
            p = i - LEAD - 1
            g_up(p).wait()
            lax.fori_loop(p * tp, (p + 1) * tp, forward, 0)
            gq_down(p).start()

        @pl.when(i >= LEAD + 2)
        def _():
            p = i - LEAD - 2
            l_down(p).wait()
            lax.fori_loop(p * tp, (p + 1) * tp, backward, 0)
            give(p)
            gq_down(p).wait()
            lax.fori_loop(p * tp, (p + 1) * tp, query_back, 0)
            for k in range(chans):
                r_send(0, p, k).start()

        return carry

    lax.fori_loop(0, pieces + LEAD + 2, stage, 0)
    later.wait()
    lax.fori_loop(0, chans * pieces * tp, beyond, 0)
    def turned(n, carry):
        p, k = n // chans, lax.rem(n, chans)
        d = owner(k)
        for t in range(tp):
            lane = pl.ds(al(p * pw + t * LANES, LANES), LANES)
            at = pl.ds(al(d * width + p * pw + t * LANES, LANES), LANES)
            top = back[:, at].astype(f32)
            end = bedge[:, at].astype(f32)
            for m in range(2):
                z = 2 * (t % 2) + m
                gs[z, pl.ds(0, rows), :] = top * kvv[1 - m, :, at]
                gs[z, pl.ds(rows, EDGE), :] = end * kvxv[1 - m, :, at]
                tap = lambda j: tapsx[d, 8 * (m + 1) + j : 8 * (m + 1) + j + 1, lane]
                total = tap(0) * gs[z, pl.ds(0, rows), :]
                for j in range(1, SHORT):
                    total = total + tap(j) * (fm[j - 1, pl.ds(j, rows), :] * gs[z, pl.ds(j, rows), :])
                    out[m + 1, :, at] = total.astype(bf)
        return carry

    def come(p, carry):
        for k in range(chans):
            if k == me:
                r_send(1, p, k).wait()
            else:
                r_send(1, p, k).wait_recv()
                e_send(p, k).wait_recv()

        @pl.when(c == chans - 1)
        def _():
            e_wrap(p).wait_recv()

        @pl.when(c < chans - 1)
        def _():
            e_send(p, me).wait()

        lax.fori_loop(p * chans, (p + 1) * chans, turned, 0)
        return carry

    lax.fori_loop(0, pieces, come, 0)

    def finish(p, carry):
        for k in range(chans):
            if k != me:
                q_send(p, k).wait_send()
                g_send(p, k).wait_send()
                r_send(1, p, k).wait_send()
                e_send(p, k).wait_send()
            r_send(0, p, k).wait()

        @pl.when(c == chans - 1)
        def _():
            e_wrap(p).wait_send()

        return carry

    lax.fori_loop(0, pieces, finish, 0)


def copy_kernel(a, b, a_out, b_out, sem):
    half = b.shape[0] // 2
    outs = [pltpu.make_async_copy(a.at[i], a_out.at[i], sem.at[i]) for i in range(3)]
    for i in range(2):
        at = pl.ds(i * half, half)
        outs.append(pltpu.make_async_copy(b.at[at], b_out.at[at], sem.at[3 + i]))
    for cp in outs:
        cp.start()
    for cp in outs:
        cp.wait()


def solution(mesh):
    chans, seqs = mesh.shape["chan"], mesh.shape["seq"]

    def body(features, cotangent, short_filter, medium_filter, doc_start):
        own, width = cotangent.shape
        rows, _, full = features.shape
        groups = medium_filter.shape[0]
        span = full // (groups * chans)
        more = rows + EDGE
        bf, f32 = jnp.bfloat16, jnp.float32
        shape = jax.ShapeDtypeStruct
        dma = lambda *dims: pltpu.SemaphoreType.DMA(dims)
        x = jnp.transpose(features, (1, 0, 2))
        ctaps = jnp.transpose(short_filter, (0, 2, 1))
        limit = 58 << 20
        tiles = width // LANES
        pieces = min(PIECES, tiles)
        blocks = own // MEDIUM
        per = LANES // span
        vm = pltpu.VMEM

        hy, grad = pl.pallas_call(
            functools.partial(core_kernel, chans, seqs, span, pieces),
            out_shape=(vm((own, width), bf), vm((3, rows, full), bf)),
            in_specs=[ANY] * 5,
            out_specs=(VMEM, VMEM),
            scratch_shapes=[
                vm((3, SHORT, groups), f32), vm((groups, MEDIUM), f32), pltpu.SMEM(doc_start.shape, jnp.int32),
                vm((rows, full), bf), vm((EDGE, full), bf), vm((chans, 24, width), f32), vm((SHORT - 1, more, LANES), f32),
                vm((2, rows, full), bf), vm((2, EDGE, full), bf), vm((2, EDGE, full), bf),
                vm((chans, 3, 8, groups), f32), vm((own, width), bf), vm((TAIL + own, width), bf),
                vm((rows, full), bf), vm((MEDIUM + own, width), bf), vm((own + MEDIUM, width), bf),
                vm((2, rows, full), f32), vm((2, EDGE, full), f32), vm((4, rows + EDGE, LANES), f32), vm((4, more, LANES), f32),
                vm((2, 2 * EDGE, LANES), f32), vm((TAIL + own, LANES), f32),
                vm((own, width), f32), vm((SHORT - 1, own + EDGE, LANES), f32),
                vm((blocks, MEDIUM, 2 * MEDIUM), bf), vm((blocks, MEDIUM, 2 * MEDIUM), bf),
                vm((blocks, per * MEDIUM, 2 * MEDIUM), bf), vm((groups, MEDIUM), f32), vm((groups, MEDIUM), f32),
                vm((2, own, width), bf), vm((own + EDGE, width), f32),
                dma(2), dma(2), dma(chans), dma(chans), dma(5),
                dma(pieces, chans), dma(pieces, chans), dma(pieces, chans), dma(pieces, chans), dma(1),
                dma(4, pieces), dma(4, pieces), dma(2, pieces, chans), dma(2, pieces, chans), dma(2, pieces),
                dma(pieces, chans), dma(pieces, chans), dma(pieces),
            ],
            compiler_params=pltpu.CompilerParams(
                collective_id=0, has_side_effects=True, vmem_limit_bytes=limit),
            name="core",
        )(x, cotangent, ctaps, medium_filter, doc_start)

        return hy, jnp.transpose(grad, (1, 0, 2))

    in_specs = (
        P(("seq", "chan"), None, None),
        P("seq", "chan"),
        P(None, "chan", None),
        P("chan", None),
        P(),
    )
    out_specs = (P("seq", "chan"), P(("seq", "chan"), None, None))
    return jax.shard_map(body, mesh=mesh, in_specs=in_specs, out_specs=out_specs, check_vma=False)
```

```python
import functools

import jax
import jax.numpy as jnp
from jax import lax
from jax.experimental import pallas as pl
from jax.experimental.pallas import tpu as pltpu
from jax.sharding import PartitionSpec as P

SHORT = 7
MEDIUM = 128
EDGE = 8
TAIL = 16
LANES = 128
PIECES = 8
AHEAD = 4
LEAD = 1
QUEUE = 4
FAR = 1 << 20
MESH = pl.DeviceIdType.MESH
ANY = pl.BlockSpec(memory_space=pl.ANY)
VMEM = pl.BlockSpec(memory_space=pltpu.VMEM)


def remote(src, dst, ssem, rsem, dev):
    return pltpu.make_async_remote_copy(src, dst, ssem, rsem, device_id=dev, device_id_type=MESH)


def al(i, n):
    return pl.multiple_of(i, n)


def split3(t):
    bf, f32 = jnp.bfloat16, jnp.float32
    high = t.astype(bf)
    rest = t - high.astype(f32)
    mid = rest.astype(bf)
    low = (rest - mid.astype(f32)).astype(bf)
    return high, mid, low


def core_kernel(chans, seqs, span, pieces, x, cot, ctaps_hbm, filt_hbm, doc_hbm, hy, out, ctaps, filt, doc,
                back, bedge, tapsx, fm, xk, xprev, xnext, tall, cotv, q, gbuf, gat, gl, kvv, kvxv, xs, gs, xe, xq, sh, fmq, mf, mb, lf, filtf, filtr, sent, gq,
                esem, fsem, tsem, trsem, lsem, qss, qrs, gss, grs, nsem, hss, hrs, rss, rrs, rls, bss, brs, bls):
    c, s = lax.axis_index("chan"), lax.axis_index("seq")
    f32, bf = jnp.float32, jnp.bfloat16
    rows = x.shape[1]
    full = x.shape[2]
    more = rows + EDGE
    own, width = cot.shape
    groups = filt.shape[0]
    pw = width // pieces
    tp = pw // LANES
    half = chans // 2
    me = chans - 2
    start = s * own

    bar = pltpu.get_barrier_semaphore()
    for k in range(1, chans):
        pl.semaphore_signal(bar, inc=1, device_id={"chan": lax.rem(c + k, chans)}, device_id_type=MESH)
    for step in (1, seqs - 1):
        for k in range(chans):
            dev = {"seq": lax.rem(s + step, seqs), "chan": lax.rem(c + k, chans)}
            pl.semaphore_signal(bar, inc=1, device_id=dev, device_id_type=MESH)
    up, down = {"seq": lax.rem(s + 1, seqs)}, {"seq": lax.rem(s + seqs - 1, seqs)}
    after = {"seq": lax.rem(s + (c + 1) // chans, seqs), "chan": lax.rem(c + 1, chans)}
    ahead = {"seq": lax.rem(s + seqs - 1 + (c + chans - 1) // chans, seqs), "chan": lax.rem(c + chans - 1, chans)}

    def owner(k):
        return lax.rem(c // 2 + 1 + k // 2, half) * 2 + lax.rem(lax.rem(c, 2) + lax.rem(k, 2), 2)

    owners = [owner(k) for k in range(chans)]
    mine = pl.ds(al(TAIL + c * rows, 16), rows)
    gmine = pl.ds(al(MEDIUM + c * rows, 16), rows)

    def cols(d, p):
        return pl.ds(al(d * width + p * pw, LANES), pw)

    def part(p):
        return pl.ds(al(p * pw, LANES), pw)

    def q_send(p, k):
        d = owners[k]
        if k == me:
            return pltpu.make_async_copy(x.at[0, :, cols(d, p)], q.at[mine, part(p)], qrs.at[p, k])
        return remote(x.at[0, :, cols(d, p)], q.at[mine, part(p)], qss.at[p, k], qrs.at[p, k], {"chan": d})

    def g_send(p, k):
        d = owners[k]
        if k == me:
            return pltpu.make_async_copy(gbuf.at[:, cols(d, p)], gat.at[gmine, part(p)], grs.at[p, k])
        return remote(gbuf.at[:, cols(d, p)], gat.at[gmine, part(p)], gss.at[p, k], grs.at[p, k], {"chan": d})

    def q_up(p):
        return remote(q.at[pl.ds(own, TAIL), part(p)], q.at[pl.ds(0, TAIL), part(p)], hss.at[0, p], hrs.at[0, p], up)

    def g_up(p):
        return remote(gat.at[pl.ds(own, MEDIUM), part(p)], gat.at[pl.ds(0, MEDIUM), part(p)], hss.at[1, p],
                      hrs.at[1, p], up)

    def l_down(p):
        return remote(gl.at[pl.ds(0, MEDIUM), part(p)], gl.at[pl.ds(own, MEDIUM), part(p)], hss.at[2, p],
                      hrs.at[2, p], down)

    def gq_down(p):
        return remote(gq.at[pl.ds(0, EDGE), part(p)], gq.at[pl.ds(own, EDGE), part(p)], hss.at[3, p], hrs.at[3, p],
                      down)

    def r_send(m, p, k):
        d = owners[k]
        src = sent.at[m, pl.ds(al(d * rows, 16), rows), part(p)]
        dst = back.at[:, cols(c, p)] if m else out.at[0, :, cols(c, p)]
        if k == me:
            return pltpu.make_async_copy(src, dst, rls.at[m, p])
        return remote(src, dst, rss.at[m, p, k], rrs.at[m, p, k], {"chan": d})

    def e_send(p, k):
        d = owners[k]
        src = sent.at[1, pl.ds(al(lax.rem(d + 1, chans) * rows, 16), EDGE), part(p)]
        dst = bedge.at[:, cols(c, p)]
        if k == me:
            return pltpu.make_async_copy(src, dst, bls.at[p])
        dev = {"seq": lax.rem(s + seqs - (d + 1) // chans, seqs), "chan": d}
        return remote(src, dst, bss.at[p, k], brs.at[p, k], dev)

    def e_wrap(p):
        dev = {"seq": lax.rem(s + seqs - 1, seqs), "chan": c}
        return remote(sent.at[1, pl.ds(0, EDGE), part(p)], bedge.at[:, cols(c, p)], bss.at[p, me], brs.at[p, me], dev)

    loads = [
        pltpu.make_async_copy(x.at[pl.ds(1, 2)], xk, lsem.at[0]),
        pltpu.make_async_copy(cot, cotv, lsem.at[1]),
    ]
    small = [
        pltpu.make_async_copy(ctaps_hbm, ctaps, lsem.at[2]),
        pltpu.make_async_copy(filt_hbm, filt, lsem.at[3]),
        pltpu.make_async_copy(doc_hbm, doc, lsem.at[4]),
    ]
    for cp in small + loads:
        cp.start()

    tall[c] = jnp.zeros(tall.shape[1:], f32)

    pl.semaphore_wait(bar, chans - 1 + 2 * chans)
    taps = []
    early = [
        remote(x.at[pl.ds(1, 2), pl.ds(rows - EDGE, EDGE)], xprev, esem.at[0], fsem.at[0], after),
    ]
    later = remote(x.at[pl.ds(1, 2), pl.ds(0, EDGE)], xnext, esem.at[1], fsem.at[1], ahead)
    for k in range(chans):
        if k != me:
            taps.append(remote(tall.at[c], tall.at[c], tsem.at[k], trsem.at[k], {"chan": owners[k]}))
    for cp in early:
        cp.start()
    for cp in small:
        cp.wait()
    tall[c, :, pl.ds(0, SHORT), :] = ctaps[...]
    for cp in taps:
        cp.start()
    for p in range(min(QUEUE, pieces)):
        for k in range(chans):
            q_send(p, k).start()

    low = jnp.maximum(s - 1, 0)
    high = jnp.minimum(s + 1, seqs - 1)
    b0 = (s - 1) * own + doc[low]
    b1 = s * own + doc[s]
    b2 = (s + 1) * own + doc[high]
    tokens = seqs * own

    def ids(pos):
        one = lambda b: jnp.where(pos >= b, 1, 0)
        seg = one(b0) + one(b1) + one(b2)
        return jnp.where(pos < 0, -1, jnp.where(pos >= tokens, FAR, seg))

    pos = start + c * rows + lax.broadcasted_iota(jnp.int32, (more, LANES), 0)
    here = ids(pos)
    for j in range(1, SHORT):
        fm[j - 1] = jnp.where(here == ids(pos - j), 1.0, 0.0)
    pos = start + lax.broadcasted_iota(jnp.int32, (own + EDGE, LANES), 0)
    here = ids(pos)
    for j in range(1, SHORT):
        fmq[j - 1] = jnp.where(here == ids(pos - j), 1.0, 0.0)
    r = lax.broadcasted_iota(jnp.int32, (MEDIUM, 2 * MEDIUM), 0)
    k2 = lax.broadcasted_iota(jnp.int32, (MEDIUM, 2 * MEDIUM), 1)
    for b in range(own // MEDIUM):
        base = start + b * MEDIUM
        here = ids(base + r)
        lag = r + MEDIUM - k2
        ok = (lag >= 0) & (lag < MEDIUM) & (here == ids(base - MEDIUM + k2))
        mf[b] = jnp.where(ok, 1.0, 0.0).astype(bf)
        lag = k2 - r
        ok = (lag >= 0) & (lag < MEDIUM) & (here == ids(base + k2))
        mb[b] = jnp.where(ok, 1.0, 0.0).astype(bf)
    rounded = filt[...].astype(bf)
    filtf[...] = rounded.astype(f32)
    ri = lax.broadcasted_iota(jnp.int32, (MEDIUM, MEDIUM), 0)
    ci = lax.broadcasted_iota(jnp.int32, (MEDIUM, MEDIUM), 1)
    turn = jnp.where(lax.rem(ri + ci, MEDIUM) == 0, 1.0, 0.0).astype(bf)
    filtr[...] = jnp.dot(rounded, turn, preferred_element_type=f32)

    for cp in taps:
        cp.wait()

    def widen(n, carry):
        at = n * pw
        row = lax.broadcasted_iota(jnp.int32, (groups, pw), 0)
        col = lax.broadcasted_iota(jnp.int32, (groups, pw), 1)
        hot = jnp.where(row == (at + col) // span, 1.0, 0.0).astype(bf)
        for d in range(chans):
            full_taps = tall[d].reshape(24, groups)
            high, mid, low3 = (jnp.dot(v, hot, preferred_element_type=f32) for v in split3(full_taps))
            tapsx[d, :, pl.ds(al(at, LANES), pw)] = high + (mid + low3)
        return carry

    lax.fori_loop(0, pieces, widen, 0)
    for cp in loads + early:
        cp.wait()

    def chunk(n, carry):
        p, k = n // chans, lax.rem(n, chans)
        d = owner(k)
        for t in range(tp):
            lane = pl.ds(al(p * pw + t * LANES, LANES), LANES)
            at = pl.ds(al(d * width + p * pw + t * LANES, LANES), LANES)
            outs = []
            for m in range(2):
                z = 2 * (t % 2) + m
                xs[z, pl.ds(0, EDGE), :] = xprev[m, :, at].astype(f32)
                xs[z, pl.ds(EDGE, rows), :] = xk[m, :, at].astype(f32)
                tap = lambda j: tapsx[d, 8 * (m + 1) + j : 8 * (m + 1) + j + 1, lane]
                total = tap(0) * xs[z, pl.ds(EDGE, rows), :]
                for j in range(1, SHORT):
                    total = total + tap(j) * (fm[j - 1, pl.ds(0, rows), :] * xs[z, pl.ds(EDGE - j, rows), :])
                kvv[m, :, at] = total
                outs.append(total)
            gbuf[:, at] = (outs[0] * outs[1]).astype(bf)
        return carry

    def rowside(p, carry):
        lax.fori_loop(p * chans, (p + 1) * chans, chunk, 0)

        @pl.when(p < AHEAD)
        def _():
            for k in range(chans):
                g_send(p, k).start()

        return carry

    lax.fori_loop(0, pieces, rowside, 0)
    later.start()

    def beyond(n, carry):
        d, at0 = n // (pieces * tp), lax.rem(n, pieces * tp)
        lane = pl.ds(al(at0 * LANES, LANES), LANES)
        at = pl.ds(al(n * LANES, LANES), LANES)
        for m in range(2):
            xe[m, pl.ds(0, EDGE), :] = xk[m, pl.ds(rows - EDGE, EDGE), at].astype(f32)
            xe[m, pl.ds(EDGE, EDGE), :] = xnext[m, :, at].astype(f32)
            tap = lambda j: tapsx[d, 8 * (m + 1) + j : 8 * (m + 1) + j + 1, lane]
            total = tap(0) * xe[m, pl.ds(EDGE, EDGE), :]
            for j in range(1, SHORT):
                total = total + tap(j) * (fm[j - 1, pl.ds(rows, EDGE), :] * xe[m, pl.ds(EDGE - j, EDGE), :])
            kvxv[m, :, at] = total
        return carry

    lane_group = lax.broadcasted_iota(jnp.int32, (MEDIUM, LANES), 1) // span
    per = LANES // span
    blocks = own // MEDIUM

    def query(t, carry):
        at = pl.ds(al(t * LANES, LANES), LANES)
        xq[...] = q[:, at].astype(f32)
        step = 64
        for lo in range(0, own, step):
            tap = lambda j: tapsx[c, j : j + 1, at]
            total = tap(0) * xq[pl.ds(TAIL + lo, step), :]
            for j in range(1, SHORT):
                total = total + tap(j) * (fmq[j - 1, pl.ds(lo, step), :] * xq[pl.ds(TAIL + lo - j, step), :])
            sh[pl.ds(lo, step), at] = total
            gl[pl.ds(lo, step), at] = (cotv[pl.ds(lo, step), at].astype(f32) * total).astype(bf)
        return carry

    def band(filters, masks):
        for g in range(per):
            row = jnp.broadcast_to(filters[g : g + 1, :], (MEDIUM, MEDIUM))
            circ = pltpu.roll(row, 0, 1, stride=1, stride_axis=0).astype(bf)
            two = jnp.concatenate([circ, circ], axis=1)
            for b in range(blocks):
                lf[b, pl.ds(g * MEDIUM, MEDIUM), :] = two * masks[b]

    def product(b, source, at):
        rhs = source[pl.ds(MEDIUM * b, 2 * MEDIUM), at]
        res = jnp.dot(lf[b], rhs, preferred_element_type=f32)
        total = res[:MEDIUM]
        for g in range(1, per):
            total = jnp.where(lane_group == g, res[g * MEDIUM : (g + 1) * MEDIUM], total)
        return total

    def forward(t, carry):
        at = pl.ds(al(t * LANES, LANES), LANES)
        band(filtr[pl.ds(al(t * per, per), per), :], mf)
        for b in range(blocks):
            long = product(b, gat, at)
            lo = pl.ds(MEDIUM * b, MEDIUM)
            hy[lo, at] = (sh[lo, at] * long).astype(bf)
            gq[lo, at] = cotv[lo, at].astype(f32) * long
        return carry

    def backward(t, carry):
        at = pl.ds(al(t * LANES, LANES), LANES)
        band(filtf[pl.ds(al(t * per, per), per), :], mb)
        for b in range(blocks):
            sent[1, pl.ds(MEDIUM * b, MEDIUM), at] = product(b, gl, at).astype(bf)
        return carry

    def query_back(t, carry):
        at = pl.ds(al(t * LANES, LANES), LANES)
        xq[pl.ds(0, own + EDGE), :] = gq[:, at]
        step = 64
        for lo in range(0, own, step):
            tap = lambda j: tapsx[c, j : j + 1, at]
            total = tap(0) * xq[pl.ds(lo, step), :]
            for j in range(1, SHORT):
                total = total + tap(j) * (fmq[j - 1, pl.ds(lo + j, step), :] * xq[pl.ds(lo + j, step), :])
            sent[0, pl.ds(lo, step), at] = total.astype(bf)
        return carry

    def edges(p):
        return [e_send(p, k) for k in range(chans) if k != me]

    def give(p):
        for k in range(chans):
            r_send(1, p, k).start()
        for cp in edges(p):
            cp.start()

        @pl.when(c == chans - 1)
        def _():
            e_wrap(p).start()

        @pl.when(c < chans - 1)
        def _():
            e_send(p, me).start()

    def stage(i, carry):
        @pl.when(i < pieces)
        def _():
            for k in range(chans):
                q_send(i, k).wait() if k == me else q_send(i, k).wait_recv()
            q_up(i).start()

        @pl.when((i >= LEAD) & (i < pieces + LEAD))
        def _():
            p = i - LEAD
            for k in range(chans):
                g_send(p, k).wait() if k == me else g_send(p, k).wait_recv()
            g_up(p).start()

        @pl.when(i + QUEUE < pieces)
        def _():
            for k in range(chans):
                q_send(i + QUEUE, k).start()

        @pl.when((i >= LEAD) & (i - LEAD + AHEAD < pieces))
        def _():
            for k in range(chans):
                g_send(i - LEAD + AHEAD, k).start()

        @pl.when((i >= 1) & (i < pieces + 1))
        def _():
            p = i - 1
            q_up(p).wait()
            lax.fori_loop(p * tp, (p + 1) * tp, query, 0)
            l_down(p).start()

        @pl.when((i >= LEAD + 1) & (i < pieces + LEAD + 1))
        def _():
            p = i - LEAD - 1
            g_up(p).wait()
            lax.fori_loop(p * tp, (p + 1) * tp, forward, 0)
            gq_down(p).start()

        @pl.when(i >= LEAD + 2)
        def _():
            p = i - LEAD - 2
            l_down(p).wait()
            lax.fori_loop(p * tp, (p + 1) * tp, backward, 0)
            give(p)
            gq_down(p).wait()
            lax.fori_loop(p * tp, (p + 1) * tp, query_back, 0)
            for k in range(chans):
                r_send(0, p, k).start()

        return carry

    lax.fori_loop(0, pieces + LEAD + 2, stage, 0)
    later.wait()
    lax.fori_loop(0, chans * pieces * tp, beyond, 0)
    def turned(n, carry):
        p, k = n // chans, lax.rem(n, chans)
        d = owner(k)
        for t in range(tp):
            lane = pl.ds(al(p * pw + t * LANES, LANES), LANES)
            at = pl.ds(al(d * width + p * pw + t * LANES, LANES), LANES)
            top = back[:, at].astype(f32)
            end = bedge[:, at].astype(f32)
            for m in range(2):
                z = 2 * (t % 2) + m
                gs[z, pl.ds(0, rows), :] = top * kvv[1 - m, :, at]
                gs[z, pl.ds(rows, EDGE), :] = end * kvxv[1 - m, :, at]
                tap = lambda j: tapsx[d, 8 * (m + 1) + j : 8 * (m + 1) + j + 1, lane]
                total = tap(0) * gs[z, pl.ds(0, rows), :]
                for j in range(1, SHORT):
                    total = total + tap(j) * (fm[j - 1, pl.ds(j, rows), :] * gs[z, pl.ds(j, rows), :])
                    out[m + 1, :, at] = total.astype(bf)
        return carry

    def come(p, carry):
        for k in range(chans):
            if k == me:
                r_send(1, p, k).wait()
            else:
                r_send(1, p, k).wait_recv()
                e_send(p, k).wait_recv()

        @pl.when(c == chans - 1)
        def _():
            e_wrap(p).wait_recv()

        @pl.when(c < chans - 1)
        def _():
            e_send(p, me).wait()

        lax.fori_loop(p * chans, (p + 1) * chans, turned, 0)
        for k in range(chans):
            r_send(0, p, k).wait()
            if k != me:
                r_send(1, p, k).wait_send()
                e_send(p, k).wait_send()

        @pl.when(c == chans - 1)
        def _():
            e_wrap(p).wait_send()

        return carry

    def sent_off(p, carry):
        for k in range(chans):
            if k != me:
                q_send(p, k).wait_send()
                g_send(p, k).wait_send()
        return carry

    lax.fori_loop(0, pieces, sent_off, 0)
    lax.fori_loop(0, pieces, come, 0)


def copy_kernel(a, b, a_out, b_out, sem):
    half = b.shape[0] // 2
    outs = [pltpu.make_async_copy(a.at[i], a_out.at[i], sem.at[i]) for i in range(3)]
    for i in range(2):
        at = pl.ds(i * half, half)
        outs.append(pltpu.make_async_copy(b.at[at], b_out.at[at], sem.at[3 + i]))
    for cp in outs:
        cp.start()
    for cp in outs:
        cp.wait()


def solution(mesh):
    chans, seqs = mesh.shape["chan"], mesh.shape["seq"]

    def body(features, cotangent, short_filter, medium_filter, doc_start):
        own, width = cotangent.shape
        rows, _, full = features.shape
        groups = medium_filter.shape[0]
        span = full // (groups * chans)
        more = rows + EDGE
        bf, f32 = jnp.bfloat16, jnp.float32
        shape = jax.ShapeDtypeStruct
        dma = lambda *dims: pltpu.SemaphoreType.DMA(dims)
        x = jnp.transpose(features, (1, 0, 2))
        ctaps = jnp.transpose(short_filter, (0, 2, 1))
        limit = 54 << 20
        tiles = width // LANES
        pieces = min(PIECES, tiles)
        blocks = own // MEDIUM
        per = LANES // span
        vm = pltpu.VMEM

        hy, grad = pl.pallas_call(
            functools.partial(core_kernel, chans, seqs, span, pieces),
            out_shape=(vm((own, width), bf), vm((3, rows, full), bf)),
            in_specs=[ANY] * 5,
            out_specs=(VMEM, VMEM),
            scratch_shapes=[
                vm((3, SHORT, groups), f32), vm((groups, MEDIUM), f32), pltpu.SMEM(doc_start.shape, jnp.int32),
                vm((rows, full), bf), vm((EDGE, full), bf), vm((chans, 24, width), f32), vm((SHORT - 1, more, LANES), f32),
                vm((2, rows, full), bf), vm((2, EDGE, full), bf), vm((2, EDGE, full), bf),
                vm((chans, 3, 8, groups), f32), vm((own, width), bf), vm((TAIL + own, width), bf),
                vm((rows, full), bf), vm((MEDIUM + own, width), bf), vm((own + MEDIUM, width), bf),
                vm((2, rows, full), f32), vm((2, EDGE, full), f32), vm((4, rows + EDGE, LANES), f32), vm((4, more, LANES), f32),
                vm((2, 2 * EDGE, LANES), f32), vm((TAIL + own, LANES), f32),
                vm((own, width), f32), vm((SHORT - 1, own + EDGE, LANES), f32),
                vm((blocks, MEDIUM, 2 * MEDIUM), bf), vm((blocks, MEDIUM, 2 * MEDIUM), bf),
                vm((blocks, per * MEDIUM, 2 * MEDIUM), bf), vm((groups, MEDIUM), f32), vm((groups, MEDIUM), f32),
                vm((2, own, width), bf), vm((own + EDGE, width), f32),
                dma(2), dma(2), dma(chans), dma(chans), dma(5),
                dma(pieces, chans), dma(pieces, chans), dma(pieces, chans), dma(pieces, chans), dma(1),
                dma(4, pieces), dma(4, pieces), dma(2, pieces, chans), dma(2, pieces, chans), dma(2, pieces),
                dma(pieces, chans), dma(pieces, chans), dma(pieces),
            ],
            compiler_params=pltpu.CompilerParams(
                collective_id=0, has_side_effects=True, vmem_limit_bytes=limit),
            name="core",
        )(x, cotangent, ctaps, medium_filter, doc_start)

        grad, hy = pl.pallas_call(
            copy_kernel,
            out_shape=(shape((3, rows, full), bf), shape((own, width), bf)),
            in_specs=[VMEM, VMEM],
            out_specs=(ANY, ANY),
            scratch_shapes=[dma(5)],
            compiler_params=pltpu.CompilerParams(vmem_limit_bytes=4 << 20),
            name="hand_out",
        )(pltpu.with_memory_space_constraint(grad, pltpu.VMEM), pltpu.with_memory_space_constraint(hy, pltpu.VMEM))
        return hy, jnp.transpose(grad, (1, 0, 2))

    in_specs = (
        P(("seq", "chan"), None, None),
        P("seq", "chan"),
        P(None, "chan", None),
        P("chan", None),
        P(),
    )
    out_specs = (P("seq", "chan"), P(("seq", "chan"), None, None))
    return jax.shard_map(body, mesh=mesh, in_specs=in_specs, out_specs=out_specs, check_vma=False)
```

```python
import functools

import jax
import jax.numpy as jnp
from jax import lax
from jax.experimental import pallas as pl
from jax.experimental.pallas import tpu as pltpu
from jax.sharding import PartitionSpec as P

SHORT = 7
MEDIUM = 128
EDGE = 8
TAIL = 16
LANES = 128
PIECES = 8
AHEAD = 4
LEAD = 0
QUEUE = 4
FAR = 1 << 20
MESH = pl.DeviceIdType.MESH
ANY = pl.BlockSpec(memory_space=pl.ANY)
VMEM = pl.BlockSpec(memory_space=pltpu.VMEM)


def remote(src, dst, ssem, rsem, dev):
    return pltpu.make_async_remote_copy(src, dst, ssem, rsem, device_id=dev, device_id_type=MESH)


def al(i, n):
    return pl.multiple_of(i, n)


def split3(t):
    bf, f32 = jnp.bfloat16, jnp.float32
    high = t.astype(bf)
    rest = t - high.astype(f32)
    mid = rest.astype(bf)
    low = (rest - mid.astype(f32)).astype(bf)
    return high, mid, low


def core_kernel(chans, seqs, span, pieces, x, cot, ctaps_hbm, filt_hbm, doc_hbm, hy, out, ctaps, filt, doc,
                back, bedge, tapsx, fm, xk, xprev, xnext, tall, cotv, q, gbuf, gat, gl, kvv, kvxv, xs, gs, xe, xq, sh, fmq, mf, mb, lf, filtf, filtr, sent, gq,
                esem, fsem, tsem, trsem, lsem, qss, qrs, gss, grs, nsem, hss, hrs, rss, rrs, rls, bss, brs, bls):
    c, s = lax.axis_index("chan"), lax.axis_index("seq")
    f32, bf = jnp.float32, jnp.bfloat16
    rows = x.shape[1]
    full = x.shape[2]
    more = rows + EDGE
    own, width = cot.shape
    groups = filt.shape[0]
    pw = width // pieces
    tp = pw // LANES
    half = chans // 2
    me = chans - 2
    start = s * own

    bar = pltpu.get_barrier_semaphore()
    for k in range(1, chans):
        pl.semaphore_signal(bar, inc=1, device_id={"chan": lax.rem(c + k, chans)}, device_id_type=MESH)
    for step in (1, seqs - 1):
        for k in range(chans):
            dev = {"seq": lax.rem(s + step, seqs), "chan": lax.rem(c + k, chans)}
            pl.semaphore_signal(bar, inc=1, device_id=dev, device_id_type=MESH)
    up, down = {"seq": lax.rem(s + 1, seqs)}, {"seq": lax.rem(s + seqs - 1, seqs)}
    after = {"seq": lax.rem(s + (c + 1) // chans, seqs), "chan": lax.rem(c + 1, chans)}
    ahead = {"seq": lax.rem(s + seqs - 1 + (c + chans - 1) // chans, seqs), "chan": lax.rem(c + chans - 1, chans)}

    def owner(k):
        return lax.rem(c // 2 + 1 + k // 2, half) * 2 + lax.rem(lax.rem(c, 2) + lax.rem(k, 2), 2)

    owners = [owner(k) for k in range(chans)]
    mine = pl.ds(al(TAIL + c * rows, 16), rows)
    gmine = pl.ds(al(MEDIUM + c * rows, 16), rows)

    def cols(d, p):
        return pl.ds(al(d * width + p * pw, LANES), pw)

    def part(p):
        return pl.ds(al(p * pw, LANES), pw)

    def q_send(p, k):
        d = owners[k]
        if k == me:
            return pltpu.make_async_copy(x.at[0, :, cols(d, p)], q.at[mine, part(p)], qrs.at[p, k])
        return remote(x.at[0, :, cols(d, p)], q.at[mine, part(p)], qss.at[p, k], qrs.at[p, k], {"chan": d})

    def g_send(p, k):
        d = owners[k]
        if k == me:
            return pltpu.make_async_copy(gbuf.at[:, cols(d, p)], gat.at[gmine, part(p)], grs.at[p, k])
        return remote(gbuf.at[:, cols(d, p)], gat.at[gmine, part(p)], gss.at[p, k], grs.at[p, k], {"chan": d})

    def q_up(p):
        return remote(q.at[pl.ds(own, TAIL), part(p)], q.at[pl.ds(0, TAIL), part(p)], hss.at[0, p], hrs.at[0, p], up)

    def g_up(p):
        return remote(gat.at[pl.ds(own, MEDIUM), part(p)], gat.at[pl.ds(0, MEDIUM), part(p)], hss.at[1, p],
                      hrs.at[1, p], up)

    def l_down(p):
        return remote(gl.at[pl.ds(0, MEDIUM), part(p)], gl.at[pl.ds(own, MEDIUM), part(p)], hss.at[2, p],
                      hrs.at[2, p], down)

    def gq_down(p):
        return remote(gq.at[pl.ds(0, EDGE), part(p)], gq.at[pl.ds(own, EDGE), part(p)], hss.at[3, p], hrs.at[3, p],
                      down)

    def r_send(m, p, k):
        d = owners[k]
        src = sent.at[m, pl.ds(al(d * rows, 16), rows), part(p)]
        dst = back.at[:, cols(c, p)] if m else out.at[0, :, cols(c, p)]
        if k == me:
            return pltpu.make_async_copy(src, dst, rls.at[m, p])
        return remote(src, dst, rss.at[m, p, k], rrs.at[m, p, k], {"chan": d})

    def e_send(p, k):
        d = owners[k]
        src = sent.at[1, pl.ds(al(lax.rem(d + 1, chans) * rows, 16), EDGE), part(p)]
        dst = bedge.at[:, cols(c, p)]
        if k == me:
            return pltpu.make_async_copy(src, dst, bls.at[p])
        dev = {"seq": lax.rem(s + seqs - (d + 1) // chans, seqs), "chan": d}
        return remote(src, dst, bss.at[p, k], brs.at[p, k], dev)

    def e_wrap(p):
        dev = {"seq": lax.rem(s + seqs - 1, seqs), "chan": c}
        return remote(sent.at[1, pl.ds(0, EDGE), part(p)], bedge.at[:, cols(c, p)], bss.at[p, me], brs.at[p, me], dev)

    loads = [
        pltpu.make_async_copy(x.at[pl.ds(1, 2)], xk, lsem.at[0]),
        pltpu.make_async_copy(cot, cotv, lsem.at[1]),
    ]
    small = [
        pltpu.make_async_copy(ctaps_hbm, ctaps, lsem.at[2]),
        pltpu.make_async_copy(filt_hbm, filt, lsem.at[3]),
        pltpu.make_async_copy(doc_hbm, doc, lsem.at[4]),
    ]
    for cp in small + loads:
        cp.start()

    tall[c] = jnp.zeros(tall.shape[1:], f32)

    pl.semaphore_wait(bar, chans - 1 + 2 * chans)
    taps = []
    early = [
        remote(x.at[pl.ds(1, 2), pl.ds(rows - EDGE, EDGE)], xprev, esem.at[0], fsem.at[0], after),
    ]
    later = remote(x.at[pl.ds(1, 2), pl.ds(0, EDGE)], xnext, esem.at[1], fsem.at[1], ahead)
    for k in range(chans):
        if k != me:
            taps.append(remote(tall.at[c], tall.at[c], tsem.at[k], trsem.at[k], {"chan": owners[k]}))
    for cp in early:
        cp.start()
    for cp in small:
        cp.wait()
    tall[c, :, pl.ds(0, SHORT), :] = ctaps[...]
    for cp in taps:
        cp.start()

    low = jnp.maximum(s - 1, 0)
    high = jnp.minimum(s + 1, seqs - 1)
    b0 = (s - 1) * own + doc[low]
    b1 = s * own + doc[s]
    b2 = (s + 1) * own + doc[high]
    tokens = seqs * own

    def ids(pos):
        one = lambda b: jnp.where(pos >= b, 1, 0)
        seg = one(b0) + one(b1) + one(b2)
        return jnp.where(pos < 0, -1, jnp.where(pos >= tokens, FAR, seg))

    pos = start + c * rows + lax.broadcasted_iota(jnp.int32, (more, LANES), 0)
    here = ids(pos)
    for j in range(1, SHORT):
        fm[j - 1] = jnp.where(here == ids(pos - j), 1.0, 0.0)
    pos = start + lax.broadcasted_iota(jnp.int32, (own + EDGE, LANES), 0)
    here = ids(pos)
    for j in range(1, SHORT):
        fmq[j - 1] = jnp.where(here == ids(pos - j), 1.0, 0.0)
    r = lax.broadcasted_iota(jnp.int32, (MEDIUM, 2 * MEDIUM), 0)
    k2 = lax.broadcasted_iota(jnp.int32, (MEDIUM, 2 * MEDIUM), 1)
    for b in range(own // MEDIUM):
        base = start + b * MEDIUM
        here = ids(base + r)
        lag = r + MEDIUM - k2
        ok = (lag >= 0) & (lag < MEDIUM) & (here == ids(base - MEDIUM + k2))
        mf[b] = jnp.where(ok, 1.0, 0.0).astype(bf)
        lag = k2 - r
        ok = (lag >= 0) & (lag < MEDIUM) & (here == ids(base + k2))
        mb[b] = jnp.where(ok, 1.0, 0.0).astype(bf)
    rounded = filt[...].astype(bf)
    filtf[...] = rounded.astype(f32)
    ri = lax.broadcasted_iota(jnp.int32, (MEDIUM, MEDIUM), 0)
    ci = lax.broadcasted_iota(jnp.int32, (MEDIUM, MEDIUM), 1)
    turn = jnp.where(lax.rem(ri + ci, MEDIUM) == 0, 1.0, 0.0).astype(bf)
    filtr[...] = jnp.dot(rounded, turn, preferred_element_type=f32)

    for p in range(min(QUEUE, pieces)):
        for k in range(chans):
            q_send(p, k).start()
    for cp in taps:
        cp.wait()

    def widen(n, carry):
        at = n * pw
        row = lax.broadcasted_iota(jnp.int32, (groups, pw), 0)
        col = lax.broadcasted_iota(jnp.int32, (groups, pw), 1)
        hot = jnp.where(row == (at + col) // span, 1.0, 0.0).astype(bf)
        for d in range(chans):
            full_taps = tall[d].reshape(24, groups)
            high, mid, low3 = (jnp.dot(v, hot, preferred_element_type=f32) for v in split3(full_taps))
            tapsx[d, :, pl.ds(al(at, LANES), pw)] = high + (mid + low3)
        return carry

    for cp in loads + early:
        cp.wait()

    def chunk(n, carry):
        p, k = n // chans, lax.rem(n, chans)
        d = owner(k)
        for t in range(tp):
            lane = pl.ds(al(p * pw + t * LANES, LANES), LANES)
            at = pl.ds(al(d * width + p * pw + t * LANES, LANES), LANES)
            outs = []
            for m in range(2):
                z = 2 * (t % 2) + m
                xs[z, pl.ds(0, EDGE), :] = xprev[m, :, at].astype(f32)
                xs[z, pl.ds(EDGE, rows), :] = xk[m, :, at].astype(f32)
                tap = lambda j: tapsx[d, 8 * (m + 1) + j : 8 * (m + 1) + j + 1, lane]
                total = tap(0) * xs[z, pl.ds(EDGE, rows), :]
                for j in range(1, SHORT):
                    total = total + tap(j) * (fm[j - 1, pl.ds(0, rows), :] * xs[z, pl.ds(EDGE - j, rows), :])
                kvv[m, :, at] = total
                outs.append(total)
            gbuf[:, at] = (outs[0] * outs[1]).astype(bf)
        return carry

    def rowside(p, carry):
        widen(p, 0)
        lax.fori_loop(p * chans, (p + 1) * chans, chunk, 0)

        @pl.when(p < AHEAD)
        def _():
            for k in range(chans):
                g_send(p, k).start()

        return carry

    lax.fori_loop(0, pieces, rowside, 0)
    later.start()

    def beyond(n, carry):
        d, at0 = n // (pieces * tp), lax.rem(n, pieces * tp)
        lane = pl.ds(al(at0 * LANES, LANES), LANES)
        at = pl.ds(al(n * LANES, LANES), LANES)
        for m in range(2):
            xe[m, pl.ds(0, EDGE), :] = xk[m, pl.ds(rows - EDGE, EDGE), at].astype(f32)
            xe[m, pl.ds(EDGE, EDGE), :] = xnext[m, :, at].astype(f32)
            tap = lambda j: tapsx[d, 8 * (m + 1) + j : 8 * (m + 1) + j + 1, lane]
            total = tap(0) * xe[m, pl.ds(EDGE, EDGE), :]
            for j in range(1, SHORT):
                total = total + tap(j) * (fm[j - 1, pl.ds(rows, EDGE), :] * xe[m, pl.ds(EDGE - j, EDGE), :])
            kvxv[m, :, at] = total
        return carry

    lane_group = lax.broadcasted_iota(jnp.int32, (MEDIUM, LANES), 1) // span
    per = LANES // span
    blocks = own // MEDIUM

    def query(t, carry):
        at = pl.ds(al(t * LANES, LANES), LANES)
        xq[...] = q[:, at].astype(f32)
        step = 64
        for lo in range(0, own, step):
            tap = lambda j: tapsx[c, j : j + 1, at]
            total = tap(0) * xq[pl.ds(TAIL + lo, step), :]
            for j in range(1, SHORT):
                total = total + tap(j) * (fmq[j - 1, pl.ds(lo, step), :] * xq[pl.ds(TAIL + lo - j, step), :])
            sh[pl.ds(lo, step), at] = total
            gl[pl.ds(lo, step), at] = (cotv[pl.ds(lo, step), at].astype(f32) * total).astype(bf)
        return carry

    def band(filters, masks):
        for g in range(per):
            row = jnp.broadcast_to(filters[g : g + 1, :], (MEDIUM, MEDIUM))
            circ = pltpu.roll(row, 0, 1, stride=1, stride_axis=0).astype(bf)
            two = jnp.concatenate([circ, circ], axis=1)
            for b in range(blocks):
                lf[b, pl.ds(g * MEDIUM, MEDIUM), :] = two * masks[b]

    def product(b, source, at):
        rhs = source[pl.ds(MEDIUM * b, 2 * MEDIUM), at]
        res = jnp.dot(lf[b], rhs, preferred_element_type=f32)
        total = res[:MEDIUM]
        for g in range(1, per):
            total = jnp.where(lane_group == g, res[g * MEDIUM : (g + 1) * MEDIUM], total)
        return total

    def forward(t, carry):
        at = pl.ds(al(t * LANES, LANES), LANES)
        band(filtr[pl.ds(al(t * per, per), per), :], mf)
        for b in range(blocks):
            long = product(b, gat, at)
            lo = pl.ds(MEDIUM * b, MEDIUM)
            hy[lo, at] = (sh[lo, at] * long).astype(bf)
            gq[lo, at] = cotv[lo, at].astype(f32) * long
        return carry

    def backward(t, carry):
        at = pl.ds(al(t * LANES, LANES), LANES)
        band(filtf[pl.ds(al(t * per, per), per), :], mb)
        for b in range(blocks):
            sent[1, pl.ds(MEDIUM * b, MEDIUM), at] = product(b, gl, at).astype(bf)
        return carry

    def query_back(t, carry):
        at = pl.ds(al(t * LANES, LANES), LANES)
        xq[pl.ds(0, own + EDGE), :] = gq[:, at]
        step = 64
        for lo in range(0, own, step):
            tap = lambda j: tapsx[c, j : j + 1, at]
            total = tap(0) * xq[pl.ds(lo, step), :]
            for j in range(1, SHORT):
                total = total + tap(j) * (fmq[j - 1, pl.ds(lo + j, step), :] * xq[pl.ds(lo + j, step), :])
            sent[0, pl.ds(lo, step), at] = total.astype(bf)
        return carry

    def edges(p):
        return [e_send(p, k) for k in range(chans) if k != me]

    def give(p):
        for k in range(chans):
            r_send(1, p, k).start()
        for cp in edges(p):
            cp.start()

        @pl.when(c == chans - 1)
        def _():
            e_wrap(p).start()

        @pl.when(c < chans - 1)
        def _():
            e_send(p, me).start()

    def stage(i, carry):
        @pl.when(i < pieces)
        def _():
            for k in range(chans):
                q_send(i, k).wait() if k == me else q_send(i, k).wait_recv()
            q_up(i).start()

        @pl.when((i >= LEAD) & (i < pieces + LEAD))
        def _():
            p = i - LEAD
            for k in range(chans):
                g_send(p, k).wait() if k == me else g_send(p, k).wait_recv()
            g_up(p).start()

        @pl.when(i + QUEUE < pieces)
        def _():
            for k in range(chans):
                q_send(i + QUEUE, k).start()

        @pl.when((i >= LEAD) & (i - LEAD + AHEAD < pieces))
        def _():
            for k in range(chans):
                g_send(i - LEAD + AHEAD, k).start()

        @pl.when((i >= 1) & (i < pieces + 1))
        def _():
            p = i - 1
            q_up(p).wait()
            lax.fori_loop(p * tp, (p + 1) * tp, query, 0)
            l_down(p).start()

        @pl.when((i >= LEAD + 1) & (i < pieces + LEAD + 1))
        def _():
            p = i - LEAD - 1
            g_up(p).wait()
            lax.fori_loop(p * tp, (p + 1) * tp, forward, 0)
            gq_down(p).start()

        @pl.when(i >= LEAD + 2)
        def _():
            p = i - LEAD - 2
            l_down(p).wait()
            lax.fori_loop(p * tp, (p + 1) * tp, backward, 0)
            give(p)
            gq_down(p).wait()
            lax.fori_loop(p * tp, (p + 1) * tp, query_back, 0)
            for k in range(chans):
                r_send(0, p, k).start()

        return carry

    lax.fori_loop(0, pieces + LEAD + 2, stage, 0)
    later.wait()
    lax.fori_loop(0, chans * pieces * tp, beyond, 0)
    def turned(n, carry):
        p, k = n // chans, lax.rem(n, chans)
        d = owner(k)
        for t in range(tp):
            lane = pl.ds(al(p * pw + t * LANES, LANES), LANES)
            at = pl.ds(al(d * width + p * pw + t * LANES, LANES), LANES)
            top = back[:, at].astype(f32)
            end = bedge[:, at].astype(f32)
            for m in range(2):
                z = 2 * (t % 2) + m
                gs[z, pl.ds(0, rows), :] = top * kvv[1 - m, :, at]
                gs[z, pl.ds(rows, EDGE), :] = end * kvxv[1 - m, :, at]
                tap = lambda j: tapsx[d, 8 * (m + 1) + j : 8 * (m + 1) + j + 1, lane]
                total = tap(0) * gs[z, pl.ds(0, rows), :]
                for j in range(1, SHORT):
                    total = total + tap(j) * (fm[j - 1, pl.ds(j, rows), :] * gs[z, pl.ds(j, rows), :])
                    out[m + 1, :, at] = total.astype(bf)
        return carry

    def come(p, carry):
        for k in range(chans):
            if k == me:
                r_send(1, p, k).wait()
            else:
                r_send(1, p, k).wait_recv()
                e_send(p, k).wait_recv()

        @pl.when(c == chans - 1)
        def _():
            e_wrap(p).wait_recv()

        @pl.when(c < chans - 1)
        def _():
            e_send(p, me).wait()

        lax.fori_loop(p * chans, (p + 1) * chans, turned, 0)
        for k in range(chans):
            r_send(0, p, k).wait()
            if k != me:
                r_send(1, p, k).wait_send()
                e_send(p, k).wait_send()

        @pl.when(c == chans - 1)
        def _():
            e_wrap(p).wait_send()

        return carry

    def sent_off(p, carry):
        for k in range(chans):
            if k != me:
                q_send(p, k).wait_send()
                g_send(p, k).wait_send()
        return carry

    lax.fori_loop(0, pieces, sent_off, 0)
    lax.fori_loop(0, pieces, come, 0)


def copy_kernel(a, b, a_out, b_out, sem):
    half = b.shape[0] // 2
    outs = [pltpu.make_async_copy(a.at[i], a_out.at[i], sem.at[i]) for i in range(3)]
    for i in range(2):
        at = pl.ds(i * half, half)
        outs.append(pltpu.make_async_copy(b.at[at], b_out.at[at], sem.at[3 + i]))
    for cp in outs:
        cp.start()
    for cp in outs:
        cp.wait()


def solution(mesh):
    chans, seqs = mesh.shape["chan"], mesh.shape["seq"]

    def body(features, cotangent, short_filter, medium_filter, doc_start):
        own, width = cotangent.shape
        rows, _, full = features.shape
        groups = medium_filter.shape[0]
        span = full // (groups * chans)
        more = rows + EDGE
        bf, f32 = jnp.bfloat16, jnp.float32
        shape = jax.ShapeDtypeStruct
        dma = lambda *dims: pltpu.SemaphoreType.DMA(dims)
        x = jnp.transpose(features, (1, 0, 2))
        ctaps = jnp.transpose(short_filter, (0, 2, 1))
        limit = 54 << 20
        tiles = width // LANES
        pieces = min(PIECES, tiles)
        blocks = own // MEDIUM
        per = LANES // span
        vm = pltpu.VMEM

        hy, grad = pl.pallas_call(
            functools.partial(core_kernel, chans, seqs, span, pieces),
            out_shape=(vm((own, width), bf), vm((3, rows, full), bf)),
            in_specs=[ANY] * 5,
            out_specs=(VMEM, VMEM),
            scratch_shapes=[
                vm((3, SHORT, groups), f32), vm((groups, MEDIUM), f32), pltpu.SMEM(doc_start.shape, jnp.int32),
                vm((rows, full), bf), vm((EDGE, full), bf), vm((chans, 24, width), f32), vm((SHORT - 1, more, LANES), f32),
                vm((2, rows, full), bf), vm((2, EDGE, full), bf), vm((2, EDGE, full), bf),
                vm((chans, 3, 8, groups), f32), vm((own, width), bf), vm((TAIL + own, width), bf),
                vm((rows, full), bf), vm((MEDIUM + own, width), bf), vm((own + MEDIUM, width), bf),
                vm((2, rows, full), f32), vm((2, EDGE, full), f32), vm((4, rows + EDGE, LANES), f32), vm((4, more, LANES), f32),
                vm((2, 2 * EDGE, LANES), f32), vm((TAIL + own, LANES), f32),
                vm((own, width), f32), vm((SHORT - 1, own + EDGE, LANES), f32),
                vm((blocks, MEDIUM, 2 * MEDIUM), bf), vm((blocks, MEDIUM, 2 * MEDIUM), bf),
                vm((blocks, per * MEDIUM, 2 * MEDIUM), bf), vm((groups, MEDIUM), f32), vm((groups, MEDIUM), f32),
                vm((2, own, width), bf), vm((own + EDGE, width), f32),
                dma(2), dma(2), dma(chans), dma(chans), dma(5),
                dma(pieces, chans), dma(pieces, chans), dma(pieces, chans), dma(pieces, chans), dma(1),
                dma(4, pieces), dma(4, pieces), dma(2, pieces, chans), dma(2, pieces, chans), dma(2, pieces),
                dma(pieces, chans), dma(pieces, chans), dma(pieces),
            ],
            compiler_params=pltpu.CompilerParams(
                collective_id=0, has_side_effects=True, vmem_limit_bytes=limit),
            name="core",
        )(x, cotangent, ctaps, medium_filter, doc_start)

        grad, hy = pl.pallas_call(
            copy_kernel,
            out_shape=(shape((3, rows, full), bf), shape((own, width), bf)),
            in_specs=[VMEM, VMEM],
            out_specs=(ANY, ANY),
            scratch_shapes=[dma(5)],
            compiler_params=pltpu.CompilerParams(vmem_limit_bytes=4 << 20),
            name="hand_out",
        )(pltpu.with_memory_space_constraint(grad, pltpu.VMEM), pltpu.with_memory_space_constraint(hy, pltpu.VMEM))
        return hy, jnp.transpose(grad, (1, 0, 2))

    in_specs = (
        P(("seq", "chan"), None, None),
        P("seq", "chan"),
        P(None, "chan", None),
        P("chan", None),
        P(),
    )
    out_specs = (P("seq", "chan"), P(("seq", "chan"), None, None))
    return jax.shard_map(body, mesh=mesh, in_specs=in_specs, out_specs=out_specs, check_vma=False)
```

```python
import functools

import jax
import jax.numpy as jnp
from jax import lax
from jax.experimental import pallas as pl
from jax.experimental.pallas import tpu as pltpu
from jax.sharding import PartitionSpec as P

SHORT = 7
MEDIUM = 128
EDGE = 8
TAIL = 16
LANES = 128
PIECES = 8
AHEAD = 4
LEAD = 0
QUEUE = 4
FAR = 1 << 20
MESH = pl.DeviceIdType.MESH
ANY = pl.BlockSpec(memory_space=pl.ANY)
VMEM = pl.BlockSpec(memory_space=pltpu.VMEM)


def remote(src, dst, ssem, rsem, dev):
    return pltpu.make_async_remote_copy(src, dst, ssem, rsem, device_id=dev, device_id_type=MESH)


def al(i, n):
    return pl.multiple_of(i, n)


def split3(t):
    bf, f32 = jnp.bfloat16, jnp.float32
    high = t.astype(bf)
    rest = t - high.astype(f32)
    mid = rest.astype(bf)
    low = (rest - mid.astype(f32)).astype(bf)
    return high, mid, low


def core_kernel(chans, seqs, span, pieces, x, cot, ctaps_hbm, filt_hbm, doc_hbm, hy, out, ctaps, filt, doc,
                back, bedge, tapsx, fm, xk, xprev, xnext, tall, cotv, q, gbuf, gat, gl, kvv, kvxv, xs, gs, xe, xq, sh, fmq, mf, mb, lf, filtf, filtr, sent, gq,
                esem, fsem, tsem, trsem, lsem, qss, qrs, gss, grs, nsem, hss, hrs, rss, rrs, rls, bss, brs, bls):
    c, s = lax.axis_index("chan"), lax.axis_index("seq")
    f32, bf = jnp.float32, jnp.bfloat16
    rows = x.shape[1]
    full = x.shape[2]
    more = rows + EDGE
    own, width = cot.shape
    groups = filt.shape[0]
    pw = width // pieces
    tp = pw // LANES
    half = chans // 2
    me = chans - 2
    start = s * own

    bar = pltpu.get_barrier_semaphore()
    for k in range(1, chans):
        pl.semaphore_signal(bar, inc=1, device_id={"chan": lax.rem(c + k, chans)}, device_id_type=MESH)
    for step in (1, seqs - 1):
        for k in range(chans):
            dev = {"seq": lax.rem(s + step, seqs), "chan": lax.rem(c + k, chans)}
            pl.semaphore_signal(bar, inc=1, device_id=dev, device_id_type=MESH)
    up, down = {"seq": lax.rem(s + 1, seqs)}, {"seq": lax.rem(s + seqs - 1, seqs)}
    after = {"seq": lax.rem(s + (c + 1) // chans, seqs), "chan": lax.rem(c + 1, chans)}
    ahead = {"seq": lax.rem(s + seqs - 1 + (c + chans - 1) // chans, seqs), "chan": lax.rem(c + chans - 1, chans)}

    def owner(k):
        return lax.rem(c // 2 + 1 + k // 2, half) * 2 + lax.rem(lax.rem(c, 2) + lax.rem(k, 2), 2)

    owners = [owner(k) for k in range(chans)]
    mine = pl.ds(al(TAIL + c * rows, 16), rows)
    gmine = pl.ds(al(MEDIUM + c * rows, 16), rows)

    def cols(d, p):
        return pl.ds(al(d * width + p * pw, LANES), pw)

    def part(p):
        return pl.ds(al(p * pw, LANES), pw)

    def q_send(p, k):
        d = owners[k]
        if k == me:
            return pltpu.make_async_copy(x.at[0, :, cols(d, p)], q.at[mine, part(p)], qrs.at[p, k])
        return remote(x.at[0, :, cols(d, p)], q.at[mine, part(p)], qss.at[p, k], qrs.at[p, k], {"chan": d})

    def g_send(p, k):
        d = owners[k]
        if k == me:
            return pltpu.make_async_copy(gbuf.at[:, cols(d, p)], gat.at[gmine, part(p)], grs.at[p, k])
        return remote(gbuf.at[:, cols(d, p)], gat.at[gmine, part(p)], gss.at[p, k], grs.at[p, k], {"chan": d})

    def q_up(p):
        return remote(q.at[pl.ds(own, TAIL), part(p)], q.at[pl.ds(0, TAIL), part(p)], hss.at[0, p], hrs.at[0, p], up)

    def g_up(p):
        return remote(gat.at[pl.ds(own, MEDIUM), part(p)], gat.at[pl.ds(0, MEDIUM), part(p)], hss.at[1, p],
                      hrs.at[1, p], up)

    def l_down(p):
        return remote(gl.at[pl.ds(0, MEDIUM), part(p)], gl.at[pl.ds(own, MEDIUM), part(p)], hss.at[2, p],
                      hrs.at[2, p], down)

    def gq_down(p):
        return remote(gq.at[pl.ds(0, EDGE), part(p)], gq.at[pl.ds(own, EDGE), part(p)], hss.at[3, p], hrs.at[3, p],
                      down)

    def r_send(m, p, k):
        d = owners[k]
        src = sent.at[m, pl.ds(al(d * rows, 16), rows), part(p)]
        dst = back.at[:, cols(c, p)] if m else out.at[0, :, cols(c, p)]
        if k == me:
            return pltpu.make_async_copy(src, dst, rls.at[m, p])
        return remote(src, dst, rss.at[m, p, k], rrs.at[m, p, k], {"chan": d})

    def e_send(p, k):
        d = owners[k]
        src = sent.at[1, pl.ds(al(lax.rem(d + 1, chans) * rows, 16), EDGE), part(p)]
        dst = bedge.at[:, cols(c, p)]
        if k == me:
            return pltpu.make_async_copy(src, dst, bls.at[p])
        dev = {"seq": lax.rem(s + seqs - (d + 1) // chans, seqs), "chan": d}
        return remote(src, dst, bss.at[p, k], brs.at[p, k], dev)

    def e_wrap(p):
        dev = {"seq": lax.rem(s + seqs - 1, seqs), "chan": c}
        return remote(sent.at[1, pl.ds(0, EDGE), part(p)], bedge.at[:, cols(c, p)], bss.at[p, me], brs.at[p, me], dev)

    loads = [
        pltpu.make_async_copy(x.at[pl.ds(1, 2)], xk, lsem.at[0]),
        pltpu.make_async_copy(cot, cotv, lsem.at[1]),
    ]
    small = [
        pltpu.make_async_copy(ctaps_hbm, ctaps, lsem.at[2]),
        pltpu.make_async_copy(filt_hbm, filt, lsem.at[3]),
        pltpu.make_async_copy(doc_hbm, doc, lsem.at[4]),
    ]
    for cp in small + loads:
        cp.start()

    tall[c] = jnp.zeros(tall.shape[1:], f32)

    pl.semaphore_wait(bar, chans - 1 + 2 * chans)
    taps = []
    early = [
        remote(x.at[pl.ds(1, 2), pl.ds(rows - EDGE, EDGE)], xprev, esem.at[0], fsem.at[0], after),
    ]
    later = remote(x.at[pl.ds(1, 2), pl.ds(0, EDGE)], xnext, esem.at[1], fsem.at[1], ahead)
    for k in range(chans):
        if k != me:
            taps.append(remote(tall.at[c], tall.at[c], tsem.at[k], trsem.at[k], {"chan": owners[k]}))
    for cp in small:
        cp.wait()
    tall[c, :, pl.ds(0, SHORT), :] = ctaps[...]
    for cp in taps:
        cp.start()
    for cp in early:
        cp.start()

    low = jnp.maximum(s - 1, 0)
    high = jnp.minimum(s + 1, seqs - 1)
    b0 = (s - 1) * own + doc[low]
    b1 = s * own + doc[s]
    b2 = (s + 1) * own + doc[high]
    tokens = seqs * own

    def ids(pos):
        one = lambda b: jnp.where(pos >= b, 1, 0)
        seg = one(b0) + one(b1) + one(b2)
        return jnp.where(pos < 0, -1, jnp.where(pos >= tokens, FAR, seg))

    pos = start + c * rows + lax.broadcasted_iota(jnp.int32, (more, LANES), 0)
    here = ids(pos)
    for j in range(1, SHORT):
        fm[j - 1] = jnp.where(here == ids(pos - j), 1.0, 0.0)
    pos = start + lax.broadcasted_iota(jnp.int32, (own + EDGE, LANES), 0)
    here = ids(pos)
    for j in range(1, SHORT):
        fmq[j - 1] = jnp.where(here == ids(pos - j), 1.0, 0.0)
    r = lax.broadcasted_iota(jnp.int32, (MEDIUM, 2 * MEDIUM), 0)
    k2 = lax.broadcasted_iota(jnp.int32, (MEDIUM, 2 * MEDIUM), 1)
    for b in range(own // MEDIUM):
        base = start + b * MEDIUM
        here = ids(base + r)
        lag = r + MEDIUM - k2
        ok = (lag >= 0) & (lag < MEDIUM) & (here == ids(base - MEDIUM + k2))
        mf[b] = jnp.where(ok, 1.0, 0.0).astype(bf)
        lag = k2 - r
        ok = (lag >= 0) & (lag < MEDIUM) & (here == ids(base + k2))
        mb[b] = jnp.where(ok, 1.0, 0.0).astype(bf)
    rounded = filt[...].astype(bf)
    filtf[...] = rounded.astype(f32)
    ri = lax.broadcasted_iota(jnp.int32, (MEDIUM, MEDIUM), 0)
    ci = lax.broadcasted_iota(jnp.int32, (MEDIUM, MEDIUM), 1)
    turn = jnp.where(lax.rem(ri + ci, MEDIUM) == 0, 1.0, 0.0).astype(bf)
    filtr[...] = jnp.dot(rounded, turn, preferred_element_type=f32)

    for p in range(min(QUEUE, pieces)):
        for k in range(chans):
            q_send(p, k).start()
    for cp in taps:
        cp.wait()

    def widen(n, carry):
        at = n * pw
        row = lax.broadcasted_iota(jnp.int32, (groups, pw), 0)
        col = lax.broadcasted_iota(jnp.int32, (groups, pw), 1)
        hot = jnp.where(row == (at + col) // span, 1.0, 0.0).astype(bf)
        for d in range(chans):
            full_taps = tall[d].reshape(24, groups)
            high, mid, low3 = (jnp.dot(v, hot, preferred_element_type=f32) for v in split3(full_taps))
            tapsx[d, :, pl.ds(al(at, LANES), pw)] = high + (mid + low3)
        return carry

    for cp in loads + early:
        cp.wait()

    def chunk(n, carry):
        p, k = n // chans, lax.rem(n, chans)
        d = owner(k)
        for t in range(tp):
            lane = pl.ds(al(p * pw + t * LANES, LANES), LANES)
            at = pl.ds(al(d * width + p * pw + t * LANES, LANES), LANES)
            outs = []
            for m in range(2):
                z = 2 * (t % 2) + m
                xs[z, pl.ds(0, EDGE), :] = xprev[m, :, at].astype(f32)
                xs[z, pl.ds(EDGE, rows), :] = xk[m, :, at].astype(f32)
                tap = lambda j: tapsx[d, 8 * (m + 1) + j : 8 * (m + 1) + j + 1, lane]
                total = tap(0) * xs[z, pl.ds(EDGE, rows), :]
                for j in range(1, SHORT):
                    total = total + tap(j) * (fm[j - 1, pl.ds(0, rows), :] * xs[z, pl.ds(EDGE - j, rows), :])
                kvv[m, :, at] = total
                outs.append(total)
            gbuf[:, at] = (outs[0] * outs[1]).astype(bf)
        return carry

    def rowside(p, carry):
        widen(p, 0)
        lax.fori_loop(p * chans, (p + 1) * chans, chunk, 0)

        @pl.when(p < AHEAD)
        def _():
            for k in range(chans):
                g_send(p, k).start()

        return carry

    lax.fori_loop(0, pieces, rowside, 0)
    later.start()

    def beyond(n, carry):
        d, at0 = n // (pieces * tp), lax.rem(n, pieces * tp)
        lane = pl.ds(al(at0 * LANES, LANES), LANES)
        at = pl.ds(al(n * LANES, LANES), LANES)
        for m in range(2):
            xe[m, pl.ds(0, EDGE), :] = xk[m, pl.ds(rows - EDGE, EDGE), at].astype(f32)
            xe[m, pl.ds(EDGE, EDGE), :] = xnext[m, :, at].astype(f32)
            tap = lambda j: tapsx[d, 8 * (m + 1) + j : 8 * (m + 1) + j + 1, lane]
            total = tap(0) * xe[m, pl.ds(EDGE, EDGE), :]
            for j in range(1, SHORT):
                total = total + tap(j) * (fm[j - 1, pl.ds(rows, EDGE), :] * xe[m, pl.ds(EDGE - j, EDGE), :])
            kvxv[m, :, at] = total
        return carry

    lane_group = lax.broadcasted_iota(jnp.int32, (MEDIUM, LANES), 1) // span
    per = LANES // span
    blocks = own // MEDIUM

    def query(t, carry):
        at = pl.ds(al(t * LANES, LANES), LANES)
        xq[...] = q[:, at].astype(f32)
        step = 64
        for lo in range(0, own, step):
            tap = lambda j: tapsx[c, j : j + 1, at]
            total = tap(0) * xq[pl.ds(TAIL + lo, step), :]
            for j in range(1, SHORT):
                total = total + tap(j) * (fmq[j - 1, pl.ds(lo, step), :] * xq[pl.ds(TAIL + lo - j, step), :])
            sh[pl.ds(lo, step), at] = total
            gl[pl.ds(lo, step), at] = (cotv[pl.ds(lo, step), at].astype(f32) * total).astype(bf)
        return carry

    def band(filters, masks):
        for g in range(per):
            row = jnp.broadcast_to(filters[g : g + 1, :], (MEDIUM, MEDIUM))
            circ = pltpu.roll(row, 0, 1, stride=1, stride_axis=0).astype(bf)
            two = jnp.concatenate([circ, circ], axis=1)
            for b in range(blocks):
                lf[b, pl.ds(g * MEDIUM, MEDIUM), :] = two * masks[b]

    def product(b, source, at):
        rhs = source[pl.ds(MEDIUM * b, 2 * MEDIUM), at]
        res = jnp.dot(lf[b], rhs, preferred_element_type=f32)
        total = res[:MEDIUM]
        for g in range(1, per):
            total = jnp.where(lane_group == g, res[g * MEDIUM : (g + 1) * MEDIUM], total)
        return total

    def forward(t, carry):
        at = pl.ds(al(t * LANES, LANES), LANES)
        band(filtr[pl.ds(al(t * per, per), per), :], mf)
        for b in range(blocks):
            long = product(b, gat, at)
            lo = pl.ds(MEDIUM * b, MEDIUM)
            hy[lo, at] = (sh[lo, at] * long).astype(bf)
            gq[lo, at] = cotv[lo, at].astype(f32) * long
        return carry

    def backward(t, carry):
        at = pl.ds(al(t * LANES, LANES), LANES)
        band(filtf[pl.ds(al(t * per, per), per), :], mb)
        for b in range(blocks):
            sent[1, pl.ds(MEDIUM * b, MEDIUM), at] = product(b, gl, at).astype(bf)
        return carry

    def query_back(t, carry):
        at = pl.ds(al(t * LANES, LANES), LANES)
        xq[pl.ds(0, own + EDGE), :] = gq[:, at]
        step = 64
        for lo in range(0, own, step):
            tap = lambda j: tapsx[c, j : j + 1, at]
            total = tap(0) * xq[pl.ds(lo, step), :]
            for j in range(1, SHORT):
                total = total + tap(j) * (fmq[j - 1, pl.ds(lo + j, step), :] * xq[pl.ds(lo + j, step), :])
            sent[0, pl.ds(lo, step), at] = total.astype(bf)
        return carry

    def edges(p):
        return [e_send(p, k) for k in range(chans) if k != me]

    def give(p):
        for k in range(chans):
            r_send(1, p, k).start()
        for cp in edges(p):
            cp.start()

        @pl.when(c == chans - 1)
        def _():
            e_wrap(p).start()

        @pl.when(c < chans - 1)
        def _():
            e_send(p, me).start()

    def stage(i, carry):
        @pl.when(i < pieces)
        def _():
            for k in range(chans):
                q_send(i, k).wait() if k == me else q_send(i, k).wait_recv()
            q_up(i).start()

        @pl.when((i >= LEAD) & (i < pieces + LEAD))
        def _():
            p = i - LEAD
            for k in range(chans):
                g_send(p, k).wait() if k == me else g_send(p, k).wait_recv()
            g_up(p).start()

        @pl.when(i + QUEUE < pieces)
        def _():
            for k in range(chans):
                q_send(i + QUEUE, k).start()

        @pl.when((i >= LEAD) & (i - LEAD + AHEAD < pieces))
        def _():
            for k in range(chans):
                g_send(i - LEAD + AHEAD, k).start()

        @pl.when((i >= 1) & (i < pieces + 1))
        def _():
            p = i - 1
            q_up(p).wait()
            lax.fori_loop(p * tp, (p + 1) * tp, query, 0)
            l_down(p).start()

        @pl.when((i >= LEAD + 1) & (i < pieces + LEAD + 1))
        def _():
            p = i - LEAD - 1
            g_up(p).wait()
            lax.fori_loop(p * tp, (p + 1) * tp, forward, 0)
            gq_down(p).start()

        @pl.when(i >= LEAD + 2)
        def _():
            p = i - LEAD - 2
            l_down(p).wait()
            lax.fori_loop(p * tp, (p + 1) * tp, backward, 0)
            give(p)
            gq_down(p).wait()
            lax.fori_loop(p * tp, (p + 1) * tp, query_back, 0)
            for k in range(chans):
                r_send(0, p, k).start()

        return carry

    lax.fori_loop(0, pieces + LEAD + 2, stage, 0)
    later.wait()
    lax.fori_loop(0, chans * pieces * tp, beyond, 0)
    def turned(n, carry):
        p, k = n // chans, lax.rem(n, chans)
        d = owner(k)
        for t in range(tp):
            lane = pl.ds(al(p * pw + t * LANES, LANES), LANES)
            at = pl.ds(al(d * width + p * pw + t * LANES, LANES), LANES)
            top = back[:, at].astype(f32)
            end = bedge[:, at].astype(f32)
            for m in range(2):
                z = 2 * (t % 2) + m
                gs[z, pl.ds(0, rows), :] = top * kvv[1 - m, :, at]
                gs[z, pl.ds(rows, EDGE), :] = end * kvxv[1 - m, :, at]
                tap = lambda j: tapsx[d, 8 * (m + 1) + j : 8 * (m + 1) + j + 1, lane]
                total = tap(0) * gs[z, pl.ds(0, rows), :]
                for j in range(1, SHORT):
                    total = total + tap(j) * (fm[j - 1, pl.ds(j, rows), :] * gs[z, pl.ds(j, rows), :])
                    out[m + 1, :, at] = total.astype(bf)
        return carry

    def come(p, carry):
        for k in range(chans):
            if k == me:
                r_send(1, p, k).wait()
            else:
                r_send(1, p, k).wait_recv()
                e_send(p, k).wait_recv()

        @pl.when(c == chans - 1)
        def _():
            e_wrap(p).wait_recv()

        @pl.when(c < chans - 1)
        def _():
            e_send(p, me).wait()

        lax.fori_loop(p * chans, (p + 1) * chans, turned, 0)
        for k in range(chans):
            r_send(0, p, k).wait()
            if k != me:
                r_send(1, p, k).wait_send()
                e_send(p, k).wait_send()

        @pl.when(c == chans - 1)
        def _():
            e_wrap(p).wait_send()

        return carry

    def sent_off(p, carry):
        for k in range(chans):
            if k != me:
                q_send(p, k).wait_send()
                g_send(p, k).wait_send()
        return carry

    lax.fori_loop(0, pieces, sent_off, 0)
    lax.fori_loop(0, pieces, come, 0)


def copy_kernel(a, b, a_out, b_out, sem):
    half = b.shape[0] // 2
    outs = [pltpu.make_async_copy(a.at[i], a_out.at[i], sem.at[i]) for i in range(3)]
    for i in range(2):
        at = pl.ds(i * half, half)
        outs.append(pltpu.make_async_copy(b.at[at], b_out.at[at], sem.at[3 + i]))
    for cp in outs:
        cp.start()
    for cp in outs:
        cp.wait()


def solution(mesh):
    chans, seqs = mesh.shape["chan"], mesh.shape["seq"]

    def body(features, cotangent, short_filter, medium_filter, doc_start):
        own, width = cotangent.shape
        rows, _, full = features.shape
        groups = medium_filter.shape[0]
        span = full // (groups * chans)
        more = rows + EDGE
        bf, f32 = jnp.bfloat16, jnp.float32
        shape = jax.ShapeDtypeStruct
        dma = lambda *dims: pltpu.SemaphoreType.DMA(dims)
        x = jnp.transpose(features, (1, 0, 2))
        ctaps = jnp.transpose(short_filter, (0, 2, 1))
        limit = 54 << 20
        tiles = width // LANES
        pieces = min(PIECES, tiles)
        blocks = own // MEDIUM
        per = LANES // span
        vm = pltpu.VMEM

        hy, grad = pl.pallas_call(
            functools.partial(core_kernel, chans, seqs, span, pieces),
            out_shape=(vm((own, width), bf), vm((3, rows, full), bf)),
            in_specs=[ANY] * 5,
            out_specs=(VMEM, VMEM),
            scratch_shapes=[
                vm((3, SHORT, groups), f32), vm((groups, MEDIUM), f32), pltpu.SMEM(doc_start.shape, jnp.int32),
                vm((rows, full), bf), vm((EDGE, full), bf), vm((chans, 24, width), f32), vm((SHORT - 1, more, LANES), f32),
                vm((2, rows, full), bf), vm((2, EDGE, full), bf), vm((2, EDGE, full), bf),
                vm((chans, 3, 8, groups), f32), vm((own, width), bf), vm((TAIL + own, width), bf),
                vm((rows, full), bf), vm((MEDIUM + own, width), bf), vm((own + MEDIUM, width), bf),
                vm((2, rows, full), f32), vm((2, EDGE, full), f32), vm((4, rows + EDGE, LANES), f32), vm((4, more, LANES), f32),
                vm((2, 2 * EDGE, LANES), f32), vm((TAIL + own, LANES), f32),
                vm((own, width), f32), vm((SHORT - 1, own + EDGE, LANES), f32),
                vm((blocks, MEDIUM, 2 * MEDIUM), bf), vm((blocks, MEDIUM, 2 * MEDIUM), bf),
                vm((blocks, per * MEDIUM, 2 * MEDIUM), bf), vm((groups, MEDIUM), f32), vm((groups, MEDIUM), f32),
                vm((2, own, width), bf), vm((own + EDGE, width), f32),
                dma(2), dma(2), dma(chans), dma(chans), dma(5),
                dma(pieces, chans), dma(pieces, chans), dma(pieces, chans), dma(pieces, chans), dma(1),
                dma(4, pieces), dma(4, pieces), dma(2, pieces, chans), dma(2, pieces, chans), dma(2, pieces),
                dma(pieces, chans), dma(pieces, chans), dma(pieces),
            ],
            compiler_params=pltpu.CompilerParams(
                collective_id=0, has_side_effects=True, vmem_limit_bytes=limit),
            name="core",
        )(x, cotangent, ctaps, medium_filter, doc_start)

        grad, hy = pl.pallas_call(
            copy_kernel,
            out_shape=(shape((3, rows, full), bf), shape((own, width), bf)),
            in_specs=[VMEM, VMEM],
            out_specs=(ANY, ANY),
            scratch_shapes=[dma(5)],
            compiler_params=pltpu.CompilerParams(vmem_limit_bytes=4 << 20),
            name="hand_out",
        )(pltpu.with_memory_space_constraint(grad, pltpu.VMEM), pltpu.with_memory_space_constraint(hy, pltpu.VMEM))
        return hy, jnp.transpose(grad, (1, 0, 2))

    in_specs = (
        P(("seq", "chan"), None, None),
        P("seq", "chan"),
        P(None, "chan", None),
        P("chan", None),
        P(),
    )
    out_specs = (P("seq", "chan"), P(("seq", "chan"), None, None))
    return jax.shard_map(body, mesh=mesh, in_specs=in_specs, out_specs=out_specs, check_vma=False)
```
